128 devices in a mesh: section: 2 (over core), seq: 16 (over z, y), head: 4 (over x).
Axes of the slice: x: 4, y: 4, z: 4, core: 2. Of those that a mesh axis runs over, the one named last changes fastest.
Arguments:
- query_vectors: bfloat16 [2, 2048, 8192], P('section', 'seq', 'head'), may hold values from -400 to 400
- key_vectors: bfloat16 [2, 2048, 8192], P('section', 'seq', 'head'), may hold values from -6 to 6
- value_vectors: bfloat16 [2, 2048, 8192], P('section', 'seq', 'head'), may hold values from -6 to 6
- prior_state: float32 [2, 64, 128, 128], P('section', 'head'), may hold values from -128 to 128
- doc_ids: int32 [2, 2048], P('section', 'seq'), may hold values from 0 to 3, never falling along the last dimension, each value on 1 to 1024 neighbouring positions
- norm_gain: float32 [2, 8192], P('section', 'head'), may hold values from 0.25 to 1.75
- residual: bfloat16 [2, 2048, 6144], P('section', 'head', 'seq'), may hold values from -6 to 6
- out_weight: bfloat16 [2, 8192, 6144], P('section', 'head', 'seq'), may hold values from -0.0625 to 0.0625
- enc_weight: bfloat16 [2, 6144, 32768], P('section', None, ('seq', 'head')), may hold values from -0.078125 to 0.078125
- enc_bias: float32 [2, 32768], P('section', ('seq', 'head')), may hold values from -5 to 5
Outputs:
- handoff: bfloat16 [2, 2048, 6144], P('section', 'head', 'seq')
- monitor: bfloat16 [2, 32, 32768], P('section', None, ('seq', 'head'))
The draws below stay inside these ranges and needn't reach their ends.
Inputs may be any that keep to these rules, and one draw needn't show every extreme that they name: `doc_ids`: document numbers never fall along a section's tokens, are 0 at its first token and rise by at most 1 from one token to the next; a document has at most 1024 tokens, and one has exactly that many.
All inputs are finite; a program needn't handle non-finite values.
Results may differ from the reference program's by a relative error of at most 0.0039.
Values may be sent and summed in bfloat16 or wider, within the bound.
No kernel may reach another device: no remote copies, remote signals or barrier semaphores. Data moves between devices by JAX's collectives and lax.ppermute only.
A program may use at most 128 MiB of HBM per device.

```python
import math
import jax
import jax.numpy as jnp
import numpy as np
from jax import lax

D = 6144
HEADS = 64
HD = 128
LAT = 32768
POOL = 64
TOK_DEV = 128
SECTIONS = 2
TOKENS = 2048
HDIM = 8192


def draw_query_vectors(key, part):
    first_key, second_key = jax.random.split(key)
    full_shape = (SECTIONS, TOKENS, HEADS * HD)
    head_number = (jnp.arange(HEADS * HD) // HD).astype(jnp.float32)
    raw_values = jnp.clip(jax.random.normal(first_key, full_shape, jnp.float32), -4.0, 4.0)
    head_scale = jnp.exp(head_number * (math.log(10.0) / HEADS))
    row_scale = jnp.exp(jax.random.uniform(second_key, (SECTIONS, TOKENS, 1), jnp.float32) * math.log(10.0))
    return (raw_values * row_scale * head_scale).astype(jnp.bfloat16)


def steps_of(key, extent, shards, smallest, largest):
    level, own = 1.0, jax.random.fold_in(key, 6)
    for position, blocks in shards:
        heights = jnp.exp(jax.random.uniform(jax.random.fold_in(own, position), (blocks,), jnp.float32, smallest / len(shards), largest / len(shards)))
        level = level * jnp.repeat(heights, extent[position] // blocks).reshape([-1 if axis == position else 1 for axis in range(len(extent))])
    return level


def length_profile(number_of, total, bound, lean):
    weights = [(1 << 20) // math.isqrt(grade ** lean) + 1 for grade in range(2, number_of + 1)]
    rest, counts = total - bound - (number_of - 1), [1] * (number_of - 1)
    while rest > 0:
        candidates = [i for i in range(number_of - 1) if counts[i] < bound]
        pool, left = sum([weights[i] for i in candidates]), rest
        for i in candidates:
            extra = min(bound - counts[i], max(1, left * weights[i] // pool), rest)
            counts[i] = counts[i] + extra
            rest = rest - extra
    return np.array([bound] + counts)


def uneven_parts(own_key, count, total, limit, slope):
    if count == 2:
        one = jax.random.randint(own_key, (), max(1, total - limit), min(limit, total - 1) + 1)
        return jnp.stack([one, total - one])
    tallies = jnp.asarray(length_profile(count, total, limit, slope), jnp.int32)
    twos = (count - 1) // 2
    donor, taker = tallies[1:1 + 2 * twos:2], tallies[2:2 + 2 * twos:2]
    margin = jnp.minimum(donor - 1, limit - taker)
    passed = jax.random.randint(jax.random.fold_in(own_key, 1), (twos,), 0, 1 << 20) % (margin + 1)
    tallies = tallies.at[1:1 + 2 * twos:2].set(donor - passed).at[2:2 + 2 * twos:2].set(taker + passed)
    return tallies[jax.random.permutation(jax.random.fold_in(own_key, 2), count)]


def scatter_about(key, extent, width, limit, cuts=(), held_as=jnp.bfloat16):
    values = width * jax.random.normal(key, extent, jnp.float32)
    if cuts:
        values = values * steps_of(key, extent, cuts, -0.22, 0.18)
    return jnp.clip(values, -limit, limit).astype(held_as)


def setup_inputs(seed: int = 0) -> dict:
    key_list = jax.random.split(jax.random.key(seed), 11)
    query_vectors = draw_query_vectors(jax.random.fold_in(key_list[10], 71), 0)
    key_vectors = scatter_about(key_list[1], (SECTIONS, TOKENS, HDIM), 1.0, 6.0, ((0, 2), (1, 16), (2, 4)))
    value_vectors = scatter_about(key_list[2], (SECTIONS, TOKENS, HDIM), 1.0, 6.0, ((0, 2), (1, 16), (2, 4)))
    prior_state = scatter_about(key_list[3], (SECTIONS, HEADS, HD, HD), ((TOKENS // 4) ** 0.5), 128.0, ((0, 2), (1, 4)), jnp.float32)
    doc_ids = jax.vmap(lambda own: jnp.searchsorted(jnp.cumsum(uneven_parts(own, 4, TOKENS, TOKENS // 2, 0)), jnp.arange(TOKENS), side="right"))(jax.random.split(key_list[4], SECTIONS)).reshape((SECTIONS, TOKENS)).astype(jnp.int32)
    norm_gain = jnp.clip(1.0 + 0.15 * jax.random.normal(key_list[5], (SECTIONS, HDIM), jnp.float32), 0.25, 1.75)
    residual = scatter_about(key_list[6], (SECTIONS, TOKENS, D), 1.0, 6.0, ((0, 2), (1, 4), (2, 16)))
    out_weight = scatter_about(key_list[7], (SECTIONS, HDIM, D), HDIM ** -0.5, 0.0625, ((0, 2), (1, 4), (2, 16)))
    enc_weight = scatter_about(key_list[8], (SECTIONS, D, LAT), D ** -0.5, 0.078125, ((0, 2), (2, 64)))
    enc_bias = scatter_about(key_list[9], (SECTIONS, LAT), 1.0, 5.0, ((0, 2), (1, 64)), jnp.float32)
    return {"query_vectors": query_vectors, "key_vectors": key_vectors, "value_vectors": value_vectors, "prior_state": prior_state, "doc_ids": doc_ids, "norm_gain": norm_gain, "residual": residual, "out_weight": out_weight, "enc_weight": enc_weight, "enc_bias": enc_bias}


epsilon = 1e-06

def merge_states(first_pair, second_pair):
    first_state, first_doc = first_pair
    second_state, second_doc = second_pair
    top_doc = jnp.maximum(first_doc, second_doc)
    merged = jnp.where(first_doc == top_doc, first_state, 0.0) + jnp.where(second_doc == top_doc, second_state, 0.0)
    return (merged, top_doc)

def attend_section(query_rows, key_rows, value_rows, prior, doc_index):
    blocks = TOKENS // TOK_DEV
    highest = lax.Precision.HIGHEST

    def shaped(array):
        return array.reshape(blocks, TOK_DEV, HEADS, HD).astype(jnp.float32)
    doc_float = doc_index.astype(jnp.float32).reshape(blocks, TOK_DEV)
    positions = jnp.arange(TOK_DEV)
    causal = positions[None, :] <= positions[:, None]

    def advance(carried, block_data):
        state, last_doc = carried
        queries_f, keys_f, values_f, docs = block_data
        inter = jnp.einsum('thd,hde->the', queries_f, state, precision=highest)
        inter = inter * (docs == last_doc).astype(jnp.float32)[:, None, None]
        scores = jnp.einsum('thd,uhd->htu', queries_f, keys_f, precision=highest)
        same_doc = causal & (docs[:, None] == docs[None, :])
        scores = jnp.where(same_doc[None, :, :], scores, 0.0)
        intra = jnp.einsum('htu,uhe->the', scores, values_f, precision=highest)
        block_last = docs[-1]
        selected = jnp.where((docs == block_last)[:, None, None], keys_f, 0.0)
        summary = jnp.einsum('thd,the->hde', selected, values_f, precision=highest)
        return (merge_states((state, last_doc), (summary, block_last)), inter + intra)
    initial = (prior.astype(jnp.float32), jnp.zeros((), jnp.float32))
    _, outputs = lax.scan(advance, initial, (shaped(query_rows), shaped(key_rows), shaped(value_rows), doc_float))
    return outputs.reshape(TOKENS, HEADS * HD)

def reference(query_vectors, key_vectors, value_vectors, prior_state, doc_ids, norm_gain, residual, out_weight, enc_weight, enc_bias):
    handoffs = []
    monitors = []
    for section_index in range(SECTIONS):
        attended = attend_section(query_vectors[section_index], key_vectors[section_index], value_vectors[section_index], prior_state[section_index], doc_ids[section_index])
        mean_square = lax.optimization_barrier(jnp.mean(attended * attended, axis=1, keepdims=True))
        normed = (attended * lax.rsqrt(mean_square + epsilon) * norm_gain[section_index]).astype(jnp.bfloat16)
        projected = jnp.dot(normed, out_weight[section_index], preferred_element_type=jnp.float32)
        layer_out = (residual[section_index].astype(jnp.float32) + projected).astype(jnp.bfloat16)
        latent = jax.nn.relu(jnp.dot(layer_out, enc_weight[section_index], preferred_element_type=jnp.float32) + enc_bias[section_index])
        pooled = lax.optimization_barrier(jnp.mean(latent.reshape(TOKENS // POOL, POOL, LAT), axis=1)).astype(jnp.bfloat16)
        handoffs.append(layer_out)
        monitors.append(pooled)
    handoff = jnp.roll(jnp.stack(handoffs), 1, axis=0)
    monitor = jnp.roll(jnp.stack(monitors), 1, axis=0)
    return (handoff, monitor)
```

```python
import functools

import jax
import jax.numpy as jnp
from jax import lax
from jax.experimental import pallas as pl
from jax.experimental.pallas import tpu as pltpu
from jax.sharding import PartitionSpec as P

HD = 128
POOL = 64
HDIM = 8192
BLK = 128
PACK = 3 * BLK + 16

epsilon = 1e-06


def dot(a, b, dims=((1,), (0,))):
    return lax.dot_general(a, b, (dims, ((), ())), preferred_element_type=jnp.float32)


def split(x):
    high = x.astype(jnp.bfloat16)
    return high, (x - high.astype(jnp.float32)).astype(jnp.bfloat16)


def attend_kernel(packed_ref, prior_ref, out_ref):
    blocks = packed_ref.shape[0]
    row = lax.broadcasted_iota(jnp.int32, (BLK, BLK), 0)
    col = lax.broadcasted_iota(jnp.int32, (BLK, BLK), 1)
    causal = col <= row
    state = prior_ref[...]
    last = jnp.zeros((BLK, BLK), jnp.float32)
    for block in range(blocks):
        queries = packed_ref[block, 0:BLK, :]
        keys = packed_ref[block, BLK : 2 * BLK, :]
        values = packed_ref[block, 2 * BLK : 3 * BLK, :]
        along = jnp.broadcast_to(
            packed_ref[block, 3 * BLK : 3 * BLK + 16, :].astype(jnp.float32)[0:1, :], (BLK, BLK)
        )
        down = along.T
        scores = dot(queries, keys, ((1,), (1,)))
        scores = jnp.where(causal & (along == down), scores, 0.0)
        high, low = split(scores)
        intra = dot(high, values) + dot(low, values)
        high, low = split(state)
        inter = dot(queries, high) + dot(queries, low)
        attended = jnp.where(down == last, inter, 0.0) + intra
        out_ref[block * BLK : (block + 1) * BLK, :] = attended.astype(out_ref.dtype)
        newest = jnp.broadcast_to(along[:, BLK - 1 :], (BLK, BLK))
        chosen = jnp.where(down == newest, keys.astype(jnp.float32), 0.0).astype(jnp.bfloat16)
        summary = dot(chosen, values, ((0,), (0,)))
        state = jnp.where(last == newest, state, 0.0) + summary
        last = newest


def attend(packed, prior):
    blocks = packed.shape[0]
    return pl.pallas_call(
        attend_kernel,
        out_shape=jax.ShapeDtypeStruct((blocks * BLK, HD), jnp.bfloat16),
        compiler_params=pltpu.CompilerParams(vmem_limit_bytes=40 << 20),
    )(packed, prior)


def project_kernel(steps, a_ref, w0, w1, w2, w3, residual_ref, out_ref, acc, square):
    step = pl.program_id(0)

    @pl.when(step == 0)
    def _():
        acc[...] = jnp.zeros_like(acc)
        square[...] = jnp.zeros_like(square)

    for i in range(a_ref.shape[0]):
        rows = slice(i * HD, (i + 1) * HD)
        a = a_ref[i]
        w = jnp.concatenate([w[rows, :] for w in (w0, w1, w2, w3)], axis=0)
        acc[...] += dot(a, w)
        wide = a.astype(jnp.float32)
        wide = wide * wide
        total = square[...]
        for j in range(wide.shape[1] // HD):
            total = total + wide[:, j * HD : (j + 1) * HD]
        square[...] = total

    @pl.when(step == steps - 1)
    def _():
        mean = jnp.sum(square[...], axis=1, keepdims=True) / HDIM
        scaled = acc[...] * lax.rsqrt(mean + epsilon)
        out_ref[...] = (residual_ref[...].astype(jnp.float32) + scaled).astype(out_ref.dtype)


def project(gathered, weights, residual, per_step=2):
    parts, rows, depth = gathered.shape
    columns = residual.shape[1]
    steps = parts // per_step
    return pl.pallas_call(
        functools.partial(project_kernel, steps),
        grid=(steps,),
        in_specs=[pl.BlockSpec((per_step, rows, depth), lambda i: (i, 0, 0))]
        + [pl.BlockSpec((per_step * HD, columns), lambda i: (i, 0))] * 4
        + [pl.BlockSpec((rows, columns), lambda i: (0, 0))],
        out_specs=pl.BlockSpec((rows, columns), lambda i: (0, 0)),
        out_shape=jax.ShapeDtypeStruct((rows, columns), jnp.bfloat16),
        scratch_shapes=[
            pltpu.VMEM((rows, columns), jnp.float32),
            pltpu.VMEM((rows, HD), jnp.float32),
        ],
        compiler_params=pltpu.CompilerParams(vmem_limit_bytes=40 << 20),
    )(gathered, *weights, residual)


def encode_kernel(steps, a_ref, e_ref, bias_ref, out_ref, acc):
    step = pl.program_id(1)
    a = jnp.concatenate([a_ref[i, 0] for i in range(a_ref.shape[0])], axis=1)
    product = dot(a, e_ref[...])

    @pl.when(step == 0)
    def _():
        acc[...] = product

    @pl.when(step > 0)
    def _():
        acc[...] += product

    @pl.when(step == steps - 1)
    def _():
        latent = jnp.maximum(acc[...] + bias_ref[...], 0.0)
        rows, width = latent.shape
        pooled = jnp.sum(latent.reshape(rows // POOL, POOL, width), axis=1) * (1.0 / POOL)
        out_ref[...] = pooled.astype(out_ref.dtype)


def encode(features, encoder, bias, per_step=4):
    parts, groups, rows, columns = features.shape
    width = encoder.shape[1]
    steps = parts // per_step
    return pl.pallas_call(
        functools.partial(encode_kernel, steps),
        grid=(groups, steps),
        in_specs=[
            pl.BlockSpec((per_step, 1, rows, columns), lambda g, i: (i, g, 0, 0)),
            pl.BlockSpec((per_step * columns, width), lambda g, i: (i, 0)),
            pl.BlockSpec((1, width), lambda g, i: (0, 0)),
        ],
        out_specs=pl.BlockSpec((rows // POOL, width), lambda g, i: (g, 0)),
        out_shape=jax.ShapeDtypeStruct((groups * rows // POOL, width), jnp.bfloat16),
        scratch_shapes=[pltpu.VMEM((rows, width), jnp.float32)],
        compiler_params=pltpu.CompilerParams(vmem_limit_bytes=40 << 20),
    )(features, encoder, bias)


def swapped(x):
    devices = lax.axis_size("section")
    return lax.ppermute(x, "section", [(i, (i + 1) % devices) for i in range(devices)])


def local(
    query_vectors,
    key_vectors,
    value_vectors,
    prior_state,
    doc_ids,
    norm_gain,
    residual,
    out_weight,
    enc_weight,
    enc_bias,
):
    groups = lax.axis_size("head")
    group, place = lax.axis_index("head"), lax.axis_index("seq")
    local_heads = query_vectors.shape[2] // HD

    def by_head(x):
        return x[0].reshape(BLK, local_heads, HD).transpose(1, 0, 2)

    docs = jnp.broadcast_to(doc_ids.astype(jnp.bfloat16)[None], (local_heads, 16, BLK))
    packed = jnp.concatenate(
        [by_head(query_vectors), by_head(key_vectors), by_head(value_vectors), docs], axis=1
    )
    packed = lax.all_to_all(packed, "seq", 0, 0, tiled=True)
    prior = lax.dynamic_index_in_dim(prior_state[0], place, 0, False)
    attended = attend(packed, prior)

    weight = (out_weight[0].astype(jnp.float32) * norm_gain[0][:, None]).astype(jnp.bfloat16)
    weights = [weight] + [
        lax.ppermute(weight, "head", [((i + k) % groups, i) for i in range(groups)])
        for k in range(1, groups)
    ]

    rows = attended.shape[0] // groups
    own = lax.all_to_all(attended.reshape(groups, rows, HD), "head", 0, 0, tiled=True)
    own = jnp.concatenate(
        [
            lax.dynamic_index_in_dim(own, (group + k) % groups, 0, False)
            for k in range(groups)
        ],
        axis=1,
    )
    layer_out = project(lax.all_gather(own, "seq"), weights, residual[0])
    features = lax.all_gather(layer_out, ("seq", "head"))
    features = features.reshape(lax.axis_size("seq"), groups, *layer_out.shape)
    pooled = encode(features, enc_weight[0], enc_bias)
    return (swapped(layer_out[None]), swapped(pooled[None]))


def solution(mesh):
    return jax.shard_map(
        local,
        mesh=mesh,
        in_specs=(
            P("section", "seq", "head"),
            P("section", "seq", "head"),
            P("section", "seq", "head"),
            P("section", "head", None, None),
            P("section", "seq"),
            P("section", "head"),
            P("section", "head", "seq"),
            P("section", "head", "seq"),
            P("section", None, ("seq", "head")),
            P("section", ("seq", "head")),
        ),
        out_specs=(P("section", "head", "seq"), P("section", None, ("seq", "head"))),
        check_vma=False,
    )
```

```python
import functools

import jax
import jax.numpy as jnp
from jax import lax
from jax.experimental import pallas as pl
from jax.experimental.pallas import tpu as pltpu
from jax.sharding import PartitionSpec as P

HD = 128
POOL = 64
HDIM = 8192
BLK = 128
PACK = 3 * BLK + 16
EXTRA = 16

epsilon = 1e-06
MIB = 1 << 20


def dot(a, b, dims=((1,), (0,))):
    return lax.dot_general(a, b, (dims, ((), ())), preferred_element_type=jnp.float32)


def split(x):
    high = x.astype(jnp.bfloat16)
    return high, (x - high.astype(jnp.float32)).astype(jnp.bfloat16)


def pack_kernel(queries_ref, keys_ref, values_ref, docs_ref, out_ref):
    docs = jnp.broadcast_to(docs_ref[...].astype(jnp.float32), (PACK - 3 * BLK, BLK))
    docs = docs.astype(out_ref.dtype)
    for head in range(out_ref.shape[0]):
        columns = slice(head * HD, (head + 1) * HD)
        out_ref[head, 0:BLK, :] = queries_ref[:, columns]
        out_ref[head, BLK : 2 * BLK, :] = keys_ref[:, columns]
        out_ref[head, 2 * BLK : 3 * BLK, :] = values_ref[:, columns]
        out_ref[head, 3 * BLK : PACK, :] = docs


def pack(queries, keys, values, docs):
    heads = queries.shape[1] // HD
    return pl.pallas_call(
        pack_kernel,
        out_shape=jax.ShapeDtypeStruct((heads, PACK, HD), jnp.bfloat16),
        compiler_params=pltpu.CompilerParams(vmem_limit_bytes=12 * MIB),
    )(queries, keys, values, docs)


def attend_kernel(packed_ref, prior_ref, gain_ref, out_ref):
    groups, per_group = out_ref.shape[0], packed_ref.shape[0] // out_ref.shape[0]
    row = lax.broadcasted_iota(jnp.int32, (BLK, BLK), 0)
    col = lax.broadcasted_iota(jnp.int32, (BLK, BLK), 1)
    causal = col <= row
    gain = gain_ref[...]
    state = prior_ref[...]
    last = jnp.zeros((BLK, BLK), jnp.float32)
    for group in range(groups):
        highs, lows = [], []
        for member in range(per_group):
            block = group * per_group + member
            queries = packed_ref[block, 0:BLK, :]
            keys = packed_ref[block, BLK : 2 * BLK, :]
            values = packed_ref[block, 2 * BLK : 3 * BLK, :]
            along = jnp.broadcast_to(
                packed_ref[block, 3 * BLK : PACK, :].astype(jnp.float32)[0:1, :], (BLK, BLK)
            )
            down = along.T
            scores = dot(queries, keys, ((1,), (1,)))
            scores = jnp.where(causal & (along == down), scores, 0.0)
            high, low = split(scores)
            intra = dot(high, values) + dot(low, values)
            high, low = split(state)
            inter = dot(queries, high) + dot(queries, low)
            attended = jnp.where(down == last, inter, 0.0) + intra
            rows = slice(member * BLK, (member + 1) * BLK)
            out_ref[group, rows, :] = (attended * gain).astype(out_ref.dtype)
            squares = jnp.sum((attended * attended).T, axis=0, keepdims=True)
            high, low = split(squares)
            highs.append(high.astype(jnp.float32))
            lows.append(low.astype(jnp.float32))
            newest = jnp.broadcast_to(along[:, BLK - 1 :], (BLK, BLK))
            chosen = jnp.where(down == newest, keys.astype(jnp.float32), 0.0)
            summary = dot(chosen.astype(jnp.bfloat16), values, ((0,), (0,)))
            state = jnp.where(last == newest, state, 0.0) + summary
            last = newest
        spare = [jnp.zeros((EXTRA - 2 * per_group, HD), jnp.float32)]
        sums = jnp.concatenate(highs + lows + spare, axis=0)
        out_ref[group, per_group * BLK :, :] = sums.astype(out_ref.dtype)


def attend(packed, prior, gain, groups):
    rows = packed.shape[0] * BLK // groups
    return pl.pallas_call(
        attend_kernel,
        out_shape=jax.ShapeDtypeStruct((groups, rows + EXTRA, HD), jnp.bfloat16),
        compiler_params=pltpu.CompilerParams(vmem_limit_bytes=12 * MIB),
    )(packed, prior, gain)


def project_kernel(steps, width, a_ref, w0, w1, w2, w3, residual_ref, out_ref, acc, square):
    step = pl.program_id(0)
    rows = residual_ref.shape[0]

    @pl.when(step == 0)
    def _():
        acc[...] = jnp.zeros_like(acc)
        square[...] = jnp.zeros_like(square)

    parts = []
    for i in range(a_ref.shape[1] // width):
        for w in (w0, w1, w2, w3):
            parts.append(w[i * HD : (i + 1) * HD, :])
    acc[...] += dot(a_ref[:rows, :], jnp.concatenate(parts, axis=0))
    sums = a_ref[rows:, :].astype(jnp.float32)
    total = square[...]
    for j in range(sums.shape[1] // HD):
        total = total + sums[:, j * HD : (j + 1) * HD]
    square[...] = total

    @pl.when(step == steps - 1)
    def _():
        blocks = rows // BLK
        for j in range(blocks):
            mean = (total[j : j + 1, :] + total[blocks + j : blocks + j + 1, :]) / HDIM
            factor = lax.rsqrt(jnp.broadcast_to(mean, (BLK, BLK)) + epsilon).T
            here = slice(j * BLK, (j + 1) * BLK)
            for c in range(acc.shape[1] // BLK):
                there = slice(c * BLK, (c + 1) * BLK)
                scaled = acc[here, there] * factor
                out_ref[here, there] = (
                    residual_ref[here, there].astype(jnp.float32) + scaled
                ).astype(out_ref.dtype)


def project(gathered, weights, residual, steps=4):
    depth = gathered.shape[1] // steps
    rows, columns = residual.shape
    return pl.pallas_call(
        functools.partial(project_kernel, steps, len(weights) * HD),
        grid=(steps,),
        in_specs=[pl.BlockSpec((rows + EXTRA, depth), lambda i: (0, i))]
        + [pl.BlockSpec((depth // len(weights), columns), lambda i: (i, 0))] * len(weights)
        + [pl.BlockSpec((rows, columns), lambda i: (0, 0))],
        out_specs=pl.BlockSpec((rows, columns), lambda i: (0, 0)),
        out_shape=jax.ShapeDtypeStruct((rows, columns), jnp.bfloat16),
        scratch_shapes=[
            pltpu.VMEM((rows, columns), jnp.float32),
            pltpu.VMEM((EXTRA, HD), jnp.float32),
        ],
        compiler_params=pltpu.CompilerParams(vmem_limit_bytes=20 * MIB),
    )(gathered, *weights, residual)


def encode_kernel(steps, a_ref, e0, e1, e2, bias_ref, out_ref, acc):
    step = pl.program_id(0)

    @pl.when(step == 0)
    def _():
        acc[...] = jnp.zeros_like(acc)

    start = 0
    for e in (e0, e1, e2):
        columns = slice(start, start + e.shape[1])
        acc[:, columns] += dot(a_ref[...], e[...])
        start += e.shape[1]

    @pl.when(step == steps - 1)
    def _():
        for i in range(out_ref.shape[0] // 8):
            pools = []
            for j in range(8 * i, 8 * i + 8):
                latent = jnp.maximum(acc[j * POOL : (j + 1) * POOL, :] + bias_ref[...], 0.0)
                pools.append(jnp.sum(latent, axis=0, keepdims=True) * (1.0 / POOL))
            out_ref[8 * i : 8 * i + 8, :] = jnp.concatenate(pools, axis=0)


def encode(features, encoders, biases, steps=8):
    rows, depth = features.shape
    width = sum(e.shape[1] for e in encoders)
    depth = depth // steps
    return pl.pallas_call(
        functools.partial(encode_kernel, steps),
        grid=(steps,),
        in_specs=[pl.BlockSpec((rows, depth), lambda i: (0, i))]
        + [pl.BlockSpec((depth, e.shape[1]), lambda i: (i, 0)) for e in encoders]
        + [pl.BlockSpec((1, width), lambda i: (0, 0))],
        out_specs=pl.BlockSpec((rows // POOL, width), lambda i: (0, 0)),
        out_shape=jax.ShapeDtypeStruct((rows // POOL, width), jnp.float32),
        scratch_shapes=[pltpu.VMEM((rows, width), jnp.float32)],
        compiler_params=pltpu.CompilerParams(vmem_limit_bytes=32 * MIB),
    )(features, *encoders, jnp.concatenate(biases, axis=1))


def local(
    query_vectors,
    key_vectors,
    value_vectors,
    prior_state,
    doc_ids,
    norm_gain,
    residual,
    out_weight,
    enc_weight,
    enc_bias,
):
    groups, sections = lax.axis_size("head"), lax.axis_size("section")
    group, place = lax.axis_index("head"), lax.axis_index("seq")

    def from_head(x, by):
        return lax.ppermute(x, "head", [((i + by) % groups, i) for i in range(groups)])

    def from_section(x, by):
        pairs = []
        for s in range(sections):
            for i in range(groups):
                target = (s + 1) % sections
                pairs.append((s * groups + (i + by) % groups, target * groups + i))
        return lax.ppermute(x, ("section", "head"), pairs)

    packed = pack(query_vectors[0], key_vectors[0], value_vectors[0], doc_ids)
    packed = lax.all_to_all(packed, "seq", 0, 0, tiled=True)
    prior = lax.dynamic_index_in_dim(prior_state[0], place, 0, False)
    gain = lax.dynamic_slice_in_dim(norm_gain, place * HD, HD, 1)
    attended = attend(packed, prior, gain, groups)

    weights = [out_weight[0]] + [from_head(out_weight[0], k) for k in range(1, groups)]
    half = enc_weight.shape[2] // 2
    encoders = [
        enc_weight[0],
        from_head(enc_weight[0][:, :half], -1),
        from_head(enc_weight[0][:, half:], 1),
    ]
    biases = [enc_bias, from_head(enc_bias[:, :half], -1), from_head(enc_bias[:, half:], 1)]

    own = lax.all_to_all(attended, "head", 0, 0, tiled=True)
    own = jnp.concatenate(
        [
            lax.dynamic_index_in_dim(own, (group + k) % groups, 0, False)
            for k in range(groups)
        ],
        axis=1,
    )
    layer_out = project(lax.all_gather(own, "seq", axis=1, tiled=True), weights, residual[0])
    both = jnp.concatenate([layer_out, from_head(layer_out, 2)], axis=0)
    features = lax.all_gather(both, "seq", axis=1, tiled=True)
    pooled = encode(features, encoders, biases).astype(jnp.bfloat16)
    pools = pooled.shape[0] // 2
    mine = from_section(pooled[:, : 2 * half], 0)
    after = from_section(pooled[:, 2 * half : 3 * half], 1)
    before = from_section(pooled[:, 3 * half :], -1)
    turned = [
        mine[:pools],
        jnp.concatenate([after[:pools], before[pools:]], axis=1),
        mine[pools:],
        jnp.concatenate([after[pools:], before[:pools]], axis=1),
    ]
    turned = jnp.stack(turned)
    monitor = jnp.concatenate(
        [
            lax.dynamic_index_in_dim(turned, (i - group) % groups, 0, False)
            for i in range(groups)
        ],
        axis=0,
    )
    return (from_section(layer_out[None], 0), monitor[None])


def solution(mesh):
    return jax.shard_map(
        local,
        mesh=mesh,
        in_specs=(
            P("section", "seq", "head"),
            P("section", "seq", "head"),
            P("section", "seq", "head"),
            P("section", "head", None, None),
            P("section", "seq"),
            P("section", "head"),
            P("section", "head", "seq"),
            P("section", "head", "seq"),
            P("section", None, ("seq", "head")),
            P("section", ("seq", "head")),
        ),
        out_specs=(P("section", "head", "seq"), P("section", None, ("seq", "head"))),
        check_vma=False,
    )
```

```python
import functools

import jax
import jax.numpy as jnp
from jax import lax
from jax.experimental import pallas as pl
from jax.experimental.pallas import tpu as pltpu
from jax.sharding import PartitionSpec as P

HD = 128
POOL = 64
HDIM = 8192
BLK = 128
PACK = 3 * BLK + 16
EXTRA = 16

epsilon = 1e-06
MIB = 1 << 20


def dot(a, b, dims=((1,), (0,))):
    return lax.dot_general(a, b, (dims, ((), ())), preferred_element_type=jnp.float32)


def split(x):
    high = x.astype(jnp.bfloat16)
    return high, (x - high.astype(jnp.float32)).astype(jnp.bfloat16)


def in_hbm(x):
    return pltpu.with_memory_space_constraint(x, pltpu.HBM)


def pack_kernel(queries_ref, keys_ref, values_ref, docs_ref, out_ref):
    docs = jnp.broadcast_to(docs_ref[...].astype(jnp.float32), (PACK - 3 * BLK, BLK))
    docs = docs.astype(out_ref.dtype)
    for head in range(out_ref.shape[0]):
        columns = slice(head * HD, (head + 1) * HD)
        out_ref[head, 0:BLK, :] = queries_ref[:, columns]
        out_ref[head, BLK : 2 * BLK, :] = keys_ref[:, columns]
        out_ref[head, 2 * BLK : 3 * BLK, :] = values_ref[:, columns]
        out_ref[head, 3 * BLK : PACK, :] = docs


def pack(queries, keys, values, docs):
    heads = queries.shape[1] // HD
    return pl.pallas_call(
        pack_kernel,
        out_shape=jax.ShapeDtypeStruct((heads, PACK, HD), jnp.bfloat16),
        compiler_params=pltpu.CompilerParams(vmem_limit_bytes=12 * MIB),
    )(*[in_hbm(x) for x in (queries, keys, values)], docs)


def attend_kernel(packed_ref, prior_ref, gain_ref, out_ref):
    groups, per_group = out_ref.shape[0], packed_ref.shape[0] // out_ref.shape[0]
    row = lax.broadcasted_iota(jnp.int32, (BLK, BLK), 0)
    col = lax.broadcasted_iota(jnp.int32, (BLK, BLK), 1)
    causal = col <= row
    gain = gain_ref[...]
    state = prior_ref[...]
    last = jnp.zeros((BLK, BLK), jnp.float32)
    for group in range(groups):
        highs, lows = [], []
        for member in range(per_group):
            block = group * per_group + member
            queries = packed_ref[block, 0:BLK, :]
            keys = packed_ref[block, BLK : 2 * BLK, :]
            values = packed_ref[block, 2 * BLK : 3 * BLK, :]
            along = jnp.broadcast_to(
                packed_ref[block, 3 * BLK : PACK, :].astype(jnp.float32)[0:1, :], (BLK, BLK)
            )
            down = along.T
            scores = dot(queries, keys, ((1,), (1,)))
            scores = jnp.where(causal & (along == down), scores, 0.0)
            high, low = split(scores)
            intra = dot(high, values) + dot(low, values)
            high, low = split(state)
            inter = dot(queries, high) + dot(queries, low)
            attended = jnp.where(down == last, inter, 0.0) + intra
            rows = slice(member * BLK, (member + 1) * BLK)
            out_ref[group, rows, :] = (attended * gain).astype(out_ref.dtype)
            squares = jnp.sum((attended * attended).T, axis=0, keepdims=True)
            high, low = split(squares)
            highs.append(high.astype(jnp.float32))
            lows.append(low.astype(jnp.float32))
            newest = jnp.broadcast_to(along[:, BLK - 1 :], (BLK, BLK))
            chosen = jnp.where(down == newest, keys.astype(jnp.float32), 0.0)
            summary = dot(chosen.astype(jnp.bfloat16), values, ((0,), (0,)))
            state = jnp.where(last == newest, state, 0.0) + summary
            last = newest
        spare = [jnp.zeros((EXTRA - 2 * per_group, HD), jnp.float32)]
        sums = jnp.concatenate(highs + lows + spare, axis=0)
        out_ref[group, per_group * BLK :, :] = sums.astype(out_ref.dtype)


def attend(packed, prior, gain, groups):
    rows = packed.shape[0] * BLK // groups
    return pl.pallas_call(
        attend_kernel,
        out_shape=jax.ShapeDtypeStruct((groups, rows + EXTRA, HD), jnp.bfloat16),
        compiler_params=pltpu.CompilerParams(vmem_limit_bytes=12 * MIB),
    )(packed, prior, gain)


def project_kernel(steps, a_ref, w0, w1, w2, w3, residual_ref, out_ref, acc, square):
    step = pl.program_id(0)
    rows = residual_ref.shape[0]

    @pl.when(step == 0)
    def _():
        acc[...] = jnp.zeros_like(acc)
        square[...] = jnp.zeros_like(square)

    total = square[...]
    for i in range(a_ref.shape[0]):
        parts = [w[i * HD : (i + 1) * HD, :] for w in (w0, w1, w2, w3)]
        acc[...] += dot(a_ref[i, :rows, :], jnp.concatenate(parts, axis=0))
        sums = a_ref[i, rows:, :].astype(jnp.float32)
        for j in range(sums.shape[1] // HD):
            total = total + sums[:, j * HD : (j + 1) * HD]
    square[...] = total

    @pl.when(step == steps - 1)
    def _():
        blocks = rows // BLK
        for j in range(blocks):
            mean = (total[j : j + 1, :] + total[blocks + j : blocks + j + 1, :]) / HDIM
            factor = lax.rsqrt(jnp.broadcast_to(mean, (BLK, BLK)) + epsilon).T
            here = slice(j * BLK, (j + 1) * BLK)
            for c in range(acc.shape[1] // BLK):
                there = slice(c * BLK, (c + 1) * BLK)
                scaled = acc[here, there] * factor
                out_ref[here, there] = (
                    residual_ref[here, there].astype(jnp.float32) + scaled
                ).astype(out_ref.dtype)


def project(gathered, weights, residual, steps=4):
    parts, _, depth = gathered.shape
    per_step = parts // steps
    rows, columns = residual.shape
    return pl.pallas_call(
        functools.partial(project_kernel, steps),
        grid=(steps,),
        in_specs=[pl.BlockSpec((per_step, rows + EXTRA, depth), lambda i: (i, 0, 0))]
        + [pl.BlockSpec((per_step * HD, columns), lambda i: (i, 0))] * len(weights)
        + [pl.BlockSpec((rows, columns), lambda i: (0, 0))],
        out_specs=pl.BlockSpec((rows, columns), lambda i: (0, 0)),
        out_shape=jax.ShapeDtypeStruct((rows, columns), jnp.bfloat16),
        scratch_shapes=[
            pltpu.VMEM((rows, columns), jnp.float32),
            pltpu.VMEM((EXTRA, HD), jnp.float32),
        ],
        compiler_params=pltpu.CompilerParams(vmem_limit_bytes=20 * MIB),
    )(in_hbm(gathered), *[in_hbm(w) for w in weights], residual)


def encode_kernel(steps, a_hbm, e0, e1, e2, bias_ref, out_ref, acc, a_buf, sems):
    step = pl.program_id(0)
    parts, rows, width = a_hbm.shape
    per_step = parts // steps

    def copies(step, slot):
        return [
            pltpu.make_async_copy(
                a_hbm.at[step * per_step + i],
                a_buf.at[slot, :, pl.ds(i * width, width)],
                sems.at[slot, i],
            )
            for i in range(per_step)
        ]

    @pl.when(step == 0)
    def _():
        for copy in copies(0, 0):
            copy.start()
        acc[...] = jnp.zeros_like(acc)

    slot = lax.rem(step, 2)

    @pl.when(step + 1 < steps)
    def _():
        for copy in copies(step + 1, 1 - slot):
            copy.start()

    for copy in copies(step, slot):
        copy.wait()
    start = 0
    for e in (e0, e1, e2):
        columns = slice(start, start + e.shape[1])
        acc[:, columns] += dot(a_buf[slot], e[...])
        start += e.shape[1]

    @pl.when(step == steps - 1)
    def _():
        for i in range(out_ref.shape[0] // 8):
            pools = []
            for j in range(8 * i, 8 * i + 8):
                latent = jnp.maximum(acc[j * POOL : (j + 1) * POOL, :] + bias_ref[...], 0.0)
                pools.append(jnp.sum(latent, axis=0, keepdims=True) * (1.0 / POOL))
            out_ref[8 * i : 8 * i + 8, :] = jnp.concatenate(pools, axis=0)


def encode(features, encoders, biases, steps=8):
    parts, rows, columns = features.shape
    width = sum(e.shape[1] for e in encoders)
    per_step = parts // steps
    depth = per_step * columns
    return pl.pallas_call(
        functools.partial(encode_kernel, steps),
        grid=(steps,),
        in_specs=[pl.BlockSpec(memory_space=pltpu.HBM)]
        + [pl.BlockSpec((depth, e.shape[1]), lambda i: (i, 0)) for e in encoders]
        + [pl.BlockSpec((1, width), lambda i: (0, 0))],
        out_specs=pl.BlockSpec((rows // POOL, width), lambda i: (0, 0)),
        out_shape=jax.ShapeDtypeStruct((rows // POOL, width), jnp.float32),
        scratch_shapes=[
            pltpu.VMEM((rows, width), jnp.float32),
            pltpu.VMEM((2, rows, depth), jnp.bfloat16),
            pltpu.SemaphoreType.DMA((2, per_step)),
        ],
        compiler_params=pltpu.CompilerParams(vmem_limit_bytes=32 * MIB),
    )(in_hbm(features), *[in_hbm(e) for e in encoders], jnp.concatenate(biases, axis=1))


def local(
    query_vectors,
    key_vectors,
    value_vectors,
    prior_state,
    doc_ids,
    norm_gain,
    residual,
    out_weight,
    enc_weight,
    enc_bias,
):
    groups, sections = lax.axis_size("head"), lax.axis_size("section")
    group, place = lax.axis_index("head"), lax.axis_index("seq")

    def from_head(x, by):
        return lax.ppermute(x, "head", [((i + by) % groups, i) for i in range(groups)])

    def from_section(x, by):
        pairs = []
        for s in range(sections):
            for i in range(groups):
                target = (s + 1) % sections
                pairs.append((s * groups + (i + by) % groups, target * groups + i))
        return lax.ppermute(x, ("section", "head"), pairs)

    packed = pack(query_vectors[0], key_vectors[0], value_vectors[0], doc_ids)
    packed = lax.all_to_all(packed, "seq", 0, 0, tiled=True)
    prior = lax.dynamic_index_in_dim(prior_state[0], place, 0, False)
    gain = lax.dynamic_slice_in_dim(norm_gain, place * HD, HD, 1)
    attended = attend(packed, prior, gain, groups)

    weights = [out_weight[0]] + [from_head(out_weight[0], k) for k in range(1, groups)]
    half = enc_weight.shape[2] // 2
    encoders = [
        enc_weight[0],
        from_head(enc_weight[0][:, :half], -1),
        from_head(enc_weight[0][:, half:], 1),
    ]
    biases = [enc_bias, from_head(enc_bias[:, :half], -1), from_head(enc_bias[:, half:], 1)]

    own = lax.all_to_all(attended, "head", 0, 0, tiled=True)
    own = jnp.concatenate(
        [
            lax.dynamic_index_in_dim(own, (group + k) % groups, 0, False)
            for k in range(groups)
        ],
        axis=1,
    )
    layer_out = project(lax.all_gather(own, "seq"), weights, residual[0])
    both = jnp.concatenate([layer_out, from_head(layer_out, 2)], axis=0)
    features = lax.all_gather(both, "seq")
    pooled = encode(features, encoders, biases).astype(jnp.bfloat16)
    pools = pooled.shape[0] // 2
    mine = from_section(pooled[:, : 2 * half], 0)
    after = from_section(pooled[:, 2 * half : 3 * half], 1)
    before = from_section(pooled[:, 3 * half :], -1)
    turned = [
        mine[:pools],
        jnp.concatenate([after[:pools], before[pools:]], axis=1),
        mine[pools:],
        jnp.concatenate([after[pools:], before[:pools]], axis=1),
    ]
    turned = jnp.stack(turned)
    monitor = jnp.concatenate(
        [
            lax.dynamic_index_in_dim(turned, (i - group) % groups, 0, False)
            for i in range(groups)
        ],
        axis=0,
    )
    return (from_section(layer_out[None], 0), monitor[None])


def solution(mesh):
    return jax.shard_map(
        local,
        mesh=mesh,
        in_specs=(
            P("section", "seq", "head"),
            P("section", "seq", "head"),
            P("section", "seq", "head"),
            P("section", "head", None, None),
            P("section", "seq"),
            P("section", "head"),
            P("section", "head", "seq"),
            P("section", "head", "seq"),
            P("section", None, ("seq", "head")),
            P("section", ("seq", "head")),
        ),
        out_specs=(P("section", "head", "seq"), P("section", None, ("seq", "head"))),
        check_vma=False,
    )
```

```python
import functools

import jax
import jax.numpy as jnp
from jax import lax
from jax.experimental import pallas as pl
from jax.experimental.pallas import tpu as pltpu
from jax.sharding import PartitionSpec as P

HD = 128
POOL = 64
HDIM = 8192
BLK = 128
PACK = 3 * BLK + 16

epsilon = 1e-06
MIB = 1 << 20


def dot(a, b, dims=((1,), (0,))):
    return lax.dot_general(a, b, (dims, ((), ())), preferred_element_type=jnp.float32)


def split(x):
    high = x.astype(jnp.bfloat16)
    return high, (x - high.astype(jnp.float32)).astype(jnp.bfloat16)


def in_hbm(x):
    return pltpu.with_memory_space_constraint(x, pltpu.HBM)


def pack_kernel(queries_ref, keys_ref, values_ref, docs_ref, out_ref):
    docs = jnp.broadcast_to(docs_ref[...].astype(jnp.float32), (PACK - 3 * BLK, BLK))
    docs = docs.astype(out_ref.dtype)
    for head in range(out_ref.shape[0]):
        columns = slice(head * HD, (head + 1) * HD)
        out_ref[head, 0:BLK, :] = queries_ref[:, columns]
        out_ref[head, BLK : 2 * BLK, :] = keys_ref[:, columns]
        out_ref[head, 2 * BLK : 3 * BLK, :] = values_ref[:, columns]
        out_ref[head, 3 * BLK : PACK, :] = docs


def pack(queries, keys, values, docs):
    heads = queries.shape[1] // HD
    return pl.pallas_call(
        pack_kernel,
        out_shape=jax.ShapeDtypeStruct((heads, PACK, HD), jnp.bfloat16),
        compiler_params=pltpu.CompilerParams(vmem_limit_bytes=12 * MIB),
    )(*[in_hbm(x) for x in (queries, keys, values)], docs)


def attend_kernel(packed_ref, prior_ref, gain_ref, out_ref):
    groups, per_group = out_ref.shape[0], packed_ref.shape[0] // out_ref.shape[0]
    row = lax.broadcasted_iota(jnp.int32, (BLK, BLK), 0)
    col = lax.broadcasted_iota(jnp.int32, (BLK, BLK), 1)
    causal = col <= row
    gain = gain_ref[...]
    state = prior_ref[...]
    last = jnp.zeros((BLK, BLK), jnp.float32)
    for group in range(groups):
        for member in range(per_group):
            block = group * per_group + member
            queries = packed_ref[block, 0:BLK, :]
            keys = packed_ref[block, BLK : 2 * BLK, :]
            values = packed_ref[block, 2 * BLK : 3 * BLK, :]
            along = jnp.broadcast_to(
                packed_ref[block, 3 * BLK : PACK, :].astype(jnp.float32)[0:1, :], (BLK, BLK)
            )
            down = along.T
            scores = dot(queries, keys, ((1,), (1,)))
            scores = jnp.where(causal & (along == down), scores, 0.0)
            high, low = split(scores)
            intra = dot(high, values) + dot(low, values)
            high, low = split(state)
            inter = dot(queries, high) + dot(queries, low)
            attended = jnp.where(down == last, inter, 0.0) + intra
            rows = slice(member * BLK, (member + 1) * BLK)
            out_ref[group, rows, :] = (attended * gain).astype(out_ref.dtype)
            newest = jnp.broadcast_to(along[:, BLK - 1 :], (BLK, BLK))
            chosen = jnp.where(down == newest, keys.astype(jnp.float32), 0.0)
            summary = dot(chosen.astype(jnp.bfloat16), values, ((0,), (0,)))
            state = jnp.where(last == newest, state, 0.0) + summary
            last = newest


def attend(packed, prior, gain, groups):
    rows = packed.shape[0] * BLK // groups
    return pl.pallas_call(
        attend_kernel,
        out_shape=jax.ShapeDtypeStruct((groups, rows, HD), jnp.bfloat16),
        compiler_params=pltpu.CompilerParams(vmem_limit_bytes=12 * MIB),
    )(packed, prior, gain)


def project_kernel(steps, final, *refs):
    source, inverse_ref, w0, w1, w2, w3 = refs[:6]
    count = 4 * len(steps)
    blocks = refs[6 : 6 + count]
    rest = refs[6 + count :]
    if final:
        acc_ref, square_ref, residual_ref, out_ref, acc, square = rest
        acc[...] = acc_ref[...]
        square[...] = square_ref[...]
    else:
        acc, square = rest
        acc[...] = jnp.zeros_like(acc)
        square[...] = jnp.zeros_like(square)

    def add(i, carry):
        across = pl.ds(pl.multiple_of(i * BLK, BLK), BLK)
        for n, step in enumerate(steps):
            for c in range(4):
                here = slice(c * BLK, (c + 1) * BLK)
                part = source[(c * 4 + step) * 4 + i]
                rows = pl.ds(pl.multiple_of(part * HD, HD), HD)
                a = blocks[n * 4 + c][across, :]
                w = jnp.concatenate([w[rows, :] for w in (w0, w1, w2, w3)], axis=0)
                acc[here, :] += dot(a, w)
                wide = a.astype(jnp.float32)
                wide = wide * wide * inverse_ref[pl.ds(part, 1), :]
                squares = square[here, :]
                for j in range(4):
                    squares += wide[:, j * HD : (j + 1) * HD]
                square[here, :] = squares
        return carry

    lax.fori_loop(0, 4, add, 0)
    if final:
        mean = jnp.sum(square[...], axis=1, keepdims=True) / HDIM
        scaled = acc[...] * lax.rsqrt(mean + epsilon)
        out_ref[...] = (residual_ref[...].astype(jnp.float32) + scaled).astype(out_ref.dtype)


def project(source, inverse, weights, rings, residual):
    rows, columns = residual.shape
    sums = [
        jax.ShapeDtypeStruct((rows, columns), jnp.float32),
        jax.ShapeDtypeStruct((rows, HD), jnp.float32),
    ]
    smem, vmem = pl.BlockSpec(memory_space=pltpu.SMEM), pl.BlockSpec(memory_space=pltpu.VMEM)

    def blocks(steps):
        return [rings[c][step] for step in steps for c in range(4)]

    early = [0, 1, 2]
    acc, square = pl.pallas_call(
        functools.partial(project_kernel, early, False),
        in_specs=[smem] + [vmem] * (5 + 4 * len(early)),
        out_specs=[vmem] * 2,
        out_shape=sums,
        compiler_params=pltpu.CompilerParams(vmem_limit_bytes=18 * MIB),
    )(source, inverse, *weights, *blocks(early))
    return pl.pallas_call(
        functools.partial(project_kernel, [3], True),
        in_specs=[smem] + [vmem] * (5 + 4 + 3),
        out_specs=vmem,
        out_shape=jax.ShapeDtypeStruct((rows, columns), jnp.bfloat16),
        scratch_shapes=[pltpu.VMEM(x.shape, x.dtype) for x in sums],
        compiler_params=pltpu.CompilerParams(vmem_limit_bytes=18 * MIB),
    )(source, inverse, *weights, *blocks([3]), acc, square, residual)


def encode_kernel(steps, first, final, *refs):
    source, e0, e1, e2 = refs[:4]
    count = 4 * len(steps)
    blocks = refs[4 : 4 + count]
    rest = refs[4 + count :]
    if final:
        acc_ref, bias_ref, out_ref, acc = rest
    elif first:
        (acc,) = rest
        acc_ref = None
    else:
        acc_ref, acc = rest
    rows, depth = blocks[0].shape[0] // 4, blocks[0].shape[1]
    acc[...] = jnp.zeros_like(acc) if first else acc_ref[...]

    def add(i, carry):
        across = pl.ds(pl.multiple_of(i * rows, BLK), rows)
        for c in range(4):
            here = slice(c * rows, (c + 1) * rows)
            start = 0
            for e in (e0, e1, e2):
                there = slice(start, start + e.shape[1])
                total = acc[here, there]
                for n, step in enumerate(steps):
                    part = source[(c * 4 + step) * 4 + i]
                    columns = pl.ds(pl.multiple_of(part * depth, BLK), depth)
                    total += dot(blocks[n * 4 + c][across, :], e[columns, :])
                acc[here, there] = total
                start += e.shape[1]
        return carry

    lax.fori_loop(0, 4, add, 0)
    if final:
        for i in range(out_ref.shape[0] // 8):
            pools = []
            for j in range(8 * i, 8 * i + 8):
                latent = jnp.maximum(acc[j * POOL : (j + 1) * POOL, :] + bias_ref[...], 0.0)
                pools.append(jnp.sum(latent, axis=0, keepdims=True) * (1.0 / POOL))
            out_ref[8 * i : 8 * i + 8, :] = jnp.concatenate(pools, axis=0)


def encode(source, encoders, rings, bias):
    rows = rings[0][0].shape[0]
    width = bias.shape[1]
    acc_shape = jax.ShapeDtypeStruct((rows, width), jnp.float32)
    smem, vmem = pl.BlockSpec(memory_space=pltpu.SMEM), pl.BlockSpec(memory_space=pltpu.VMEM)

    def blocks(steps):
        return [rings[c][step] for step in steps for c in range(4)]

    acc = None
    for steps in ([0, 1], [2]):
        acc = pl.pallas_call(
            functools.partial(encode_kernel, steps, acc is None, False),
            in_specs=[smem] + [vmem] * (3 + 4 * len(steps) + (acc is not None)),
            out_specs=vmem,
            out_shape=acc_shape,
            compiler_params=pltpu.CompilerParams(vmem_limit_bytes=28 * MIB),
        )(source, *encoders, *blocks(steps), *([] if acc is None else [acc]))
    return pl.pallas_call(
        functools.partial(encode_kernel, [3], False, True),
        in_specs=[smem] + [vmem] * (3 + 4 + 2),
        out_specs=vmem,
        out_shape=jax.ShapeDtypeStruct((rows // POOL, width), jnp.float32),
        scratch_shapes=[pltpu.VMEM(acc_shape.shape, acc_shape.dtype)],
        compiler_params=pltpu.CompilerParams(vmem_limit_bytes=28 * MIB),
    )(source, *encoders, *blocks([3]), acc, bias)


SIDE = 4
ROUTES = ((("y", 1), ("z", 1)), (("y", -1), ("z", -1)), (("z", 1), ("y", 1)), (("z", -1), ("y", -1)))


def moved(x, axis, by):
    pairs = []
    for z in range(SIDE):
        for y in range(SIDE):
            to = (z, (y + by) % SIDE) if axis == "y" else ((z + by) % SIDE, y)
            pairs.append((z * SIDE + y, to[0] * SIDE + to[1]))
    return lax.ppermute(x, "seq", pairs)


def sources(place):
    z, y = place // SIDE, place % SIDE
    table = []
    for (axis, by), (_, by_second) in ROUTES:
        for second in range(SIDE):
            for first in range(SIDE):
                back = (first * by, second * by_second)
                back_y, back_z = back if axis == "y" else back[::-1]
                table.append((z - back_z) % SIDE * SIDE + (y - back_y) % SIDE)
    return jnp.stack(table).astype(jnp.int32)


def ring_gather(quarters):
    lines = [[q] for q in quarters]
    for _ in range(SIDE - 1):
        for line, ((axis, by), _) in zip(lines, ROUTES):
            line.append(moved(line[-1], axis, by))
    rings = [[jnp.concatenate(line, axis=0)] for line in lines]
    for _ in range(SIDE - 1):
        for ring, (_, (axis, by)) in zip(rings, ROUTES):
            ring.append(moved(ring[-1], axis, by))
    return rings


def local(
    query_vectors,
    key_vectors,
    value_vectors,
    prior_state,
    doc_ids,
    norm_gain,
    residual,
    out_weight,
    enc_weight,
    enc_bias,
):
    groups, sections = lax.axis_size("head"), lax.axis_size("section")
    group, place = lax.axis_index("head"), lax.axis_index("seq")

    def from_head(x, by):
        return lax.ppermute(x, "head", [((i + by) % groups, i) for i in range(groups)])

    def from_section(x, by):
        pairs = []
        for s in range(sections):
            for i in range(groups):
                target = (s + 1) % sections
                pairs.append((s * groups + (i + by) % groups, target * groups + i))
        return lax.ppermute(x, ("section", "head"), pairs)

    packed = pack(query_vectors[0], key_vectors[0], value_vectors[0], doc_ids)
    weight = out_weight[0]
    after, before = from_head(weight, 1), from_head(weight, -1)
    gains = [norm_gain] + [from_head(norm_gain, k) for k in range(1, groups)]
    inverse = jnp.concatenate([(1.0 / (g * g)).reshape(-1, HD) for g in gains], axis=1)
    half = enc_weight.shape[2] // 2
    bias = jnp.concatenate(
        [enc_bias, from_head(enc_bias[:, :half], -1), from_head(enc_bias[:, half:], 1)], axis=1
    )
    source = sources(place)

    packed = lax.all_to_all(packed, "seq", 0, 0, tiled=True)
    prior = lax.dynamic_index_in_dim(prior_state[0], place, 0, False)
    gain = lax.dynamic_slice_in_dim(norm_gain, place * HD, HD, 1)
    attended = attend(packed, prior, gain, groups)
    attended, after, before, inverse, bias = lax.optimization_barrier(
        (attended, after, before, inverse, bias)
    )

    middle = weight.shape[0] // 2
    across = [from_head(after[:middle], 1), from_head(before[middle:], -1)]
    own = lax.all_to_all(attended, "head", 0, 0, tiled=True)
    own = jnp.concatenate(
        [
            lax.dynamic_index_in_dim(own, (group + k) % groups, 0, False)
            for k in range(groups)
        ],
        axis=1,
    )
    own, first_half = lax.optimization_barrier((own, enc_weight[0][:, :half]))
    from_before = from_head(first_half, -1)
    rings = ring_gather([own[c * BLK : (c + 1) * BLK] for c in range(4)])
    weights = [weight, after, jnp.concatenate(across, axis=0), before]
    layer_out = project(source, inverse, weights, rings, residual[0])

    layer_out, from_before, second_half = lax.optimization_barrier(
        (layer_out, from_before, enc_weight[0][:, half:])
    )
    from_after = from_head(second_half, 1)
    opposite = from_head(layer_out, 2)
    rows = layer_out.shape[0] // 2
    rings = ring_gather([layer_out[:rows], layer_out[rows:], opposite[:rows], opposite[rows:]])
    pooled = encode(source, [enc_weight[0], from_before, from_after], rings, bias)
    pooled = pooled.astype(jnp.bfloat16)
    pools = pooled.shape[0] // 2
    mine = from_section(pooled[:, : 2 * half], 0)
    after = from_section(pooled[:, 2 * half : 3 * half], 1)
    before = from_section(pooled[:, 3 * half :], -1)
    turned = [
        mine[:pools],
        jnp.concatenate([after[:pools], before[pools:]], axis=1),
        mine[pools:],
        jnp.concatenate([after[pools:], before[:pools]], axis=1),
    ]
    turned = jnp.stack(turned)
    monitor = jnp.concatenate(
        [
            lax.dynamic_index_in_dim(turned, (i - group) % groups, 0, False)
            for i in range(groups)
        ],
        axis=0,
    )
    return (from_section(layer_out[None], 0), monitor[None])


def solution(mesh):
    return jax.shard_map(
        local,
        mesh=mesh,
        in_specs=(
            P("section", "seq", "head"),
            P("section", "seq", "head"),
            P("section", "seq", "head"),
            P("section", "head", None, None),
            P("section", "seq"),
            P("section", "head"),
            P("section", "head", "seq"),
            P("section", "head", "seq"),
            P("section", None, ("seq", "head")),
            P("section", ("seq", "head")),
        ),
        out_specs=(P("section", "head", "seq"), P("section", None, ("seq", "head"))),
        check_vma=False,
    )
```

```python
import functools

import jax
import jax.numpy as jnp
from jax import lax
from jax.experimental import pallas as pl
from jax.experimental.pallas import tpu as pltpu
from jax.sharding import PartitionSpec as P

HD = 128
POOL = 64
HDIM = 8192
BLK = 128
PACK = 3 * BLK + 16

epsilon = 1e-06
MIB = 1 << 20


def dot(a, b, dims=((1,), (0,))):
    return lax.dot_general(a, b, (dims, ((), ())), preferred_element_type=jnp.float32)


def split(x):
    high = x.astype(jnp.bfloat16)
    return high, (x - high.astype(jnp.float32)).astype(jnp.bfloat16)


def in_hbm(x):
    return pltpu.with_memory_space_constraint(x, pltpu.HBM)


def pack_kernel(queries_ref, keys_ref, values_ref, docs_ref, out_ref):
    docs = jnp.broadcast_to(docs_ref[...].astype(jnp.float32), (PACK - 3 * BLK, BLK))
    docs = docs.astype(out_ref.dtype)
    for head in range(out_ref.shape[0]):
        columns = slice(head * HD, (head + 1) * HD)
        out_ref[head, 0:BLK, :] = queries_ref[:, columns]
        out_ref[head, BLK : 2 * BLK, :] = keys_ref[:, columns]
        out_ref[head, 2 * BLK : 3 * BLK, :] = values_ref[:, columns]
        out_ref[head, 3 * BLK : PACK, :] = docs


def pack(queries, keys, values, docs):
    heads = queries.shape[1] // HD
    return pl.pallas_call(
        pack_kernel,
        out_shape=jax.ShapeDtypeStruct((heads, PACK, HD), jnp.bfloat16),
        compiler_params=pltpu.CompilerParams(vmem_limit_bytes=12 * MIB),
    )(*[in_hbm(x) for x in (queries, keys, values)], docs)


def attend_kernel(packed_ref, prior_ref, gain_ref, out_ref):
    groups, per_group = out_ref.shape[0], packed_ref.shape[0] // out_ref.shape[0]
    row = lax.broadcasted_iota(jnp.int32, (BLK, BLK), 0)
    col = lax.broadcasted_iota(jnp.int32, (BLK, BLK), 1)
    causal = col <= row
    gain = gain_ref[...]
    state = prior_ref[...]
    last = jnp.zeros((BLK, BLK), jnp.float32)
    for group in range(groups):
        for member in range(per_group):
            block = group * per_group + member
            queries = packed_ref[block, 0:BLK, :]
            keys = packed_ref[block, BLK : 2 * BLK, :]
            values = packed_ref[block, 2 * BLK : 3 * BLK, :]
            along = jnp.broadcast_to(
                packed_ref[block, 3 * BLK : PACK, :].astype(jnp.float32)[0:1, :], (BLK, BLK)
            )
            down = along.T
            scores = dot(queries, keys, ((1,), (1,)))
            scores = jnp.where(causal & (along == down), scores, 0.0)
            high, low = split(scores)
            intra = dot(high, values) + dot(low, values)
            high, low = split(state)
            inter = dot(queries, high) + dot(queries, low)
            attended = jnp.where(down == last, inter, 0.0) + intra
            rows = slice(member * BLK, (member + 1) * BLK)
            out_ref[group, rows, :] = (attended * gain).astype(out_ref.dtype)
            newest = jnp.broadcast_to(along[:, BLK - 1 :], (BLK, BLK))
            chosen = jnp.where(down == newest, keys.astype(jnp.float32), 0.0)
            summary = dot(chosen.astype(jnp.bfloat16), values, ((0,), (0,)))
            state = jnp.where(last == newest, state, 0.0) + summary
            last = newest


def attend(packed, prior, gain, groups):
    rows = packed.shape[0] * BLK // groups
    return pl.pallas_call(
        attend_kernel,
        out_shape=jax.ShapeDtypeStruct((groups, rows, HD), jnp.bfloat16),
        compiler_params=pltpu.CompilerParams(vmem_limit_bytes=12 * MIB),
    )(packed, prior, gain)


def listed(gathered, steps):
    arrays, layout = [], []
    for step in steps:
        for half, parts in enumerate(gathered):
            first = 0
            for array in parts[step]:
                count = 4 * array.shape[0] // parts[0][0].shape[0]
                arrays.append(array)
                layout.append((half, step, first, count))
                first += count
    return arrays, layout


def each_part(source, layout, blocks, rows, body):
    for (half, step, first, count), block in zip(layout, blocks):

        def one(i, carry, half=half, step=step, first=first, block=block):
            part = source[(half * 4 + step) * 4 + first + i]
            across = pl.ds(pl.multiple_of(i * rows, BLK), rows)
            body(slice(half * rows, (half + 1) * rows), part, block[across, :], step)
            return carry

        lax.fori_loop(0, count, one, 0)


def project_kernel(layout, final, *refs):
    source, inverse_ref, w0, w1, w2, w3, w4 = refs[:7]
    blocks = refs[7 : 7 + len(layout)]
    rest = refs[7 + len(layout) :]
    if final:
        acc_ref, square_ref, residual_ref, out_ref, acc, square = rest
        acc[...] = acc_ref[...]
        square[...] = square_ref[...]
    else:
        acc, square = rest
        acc[...] = jnp.zeros_like(acc)
        square[...] = jnp.zeros_like(square)
    middle = w2.shape[0] // HD

    def body(here, part, a, step):
        rows = pl.ds(pl.multiple_of(part * HD, HD), HD)
        inner = pl.ds(pl.multiple_of(lax.rem(part, middle) * HD, HD), HD)
        lower = (part < middle).astype(jnp.float32)
        far = w2[inner, :].astype(jnp.float32) * lower
        far = far + w3[inner, :].astype(jnp.float32) * (1.0 - lower)
        w = jnp.concatenate([w0[rows, :], w1[rows, :], far.astype(w0.dtype), w4[rows, :]], axis=0)
        acc[here, :] += dot(a, w)
        wide = a.astype(jnp.float32)
        wide = wide * wide * inverse_ref[pl.ds(part, 1), :]
        squares = square[here, :]
        for j in range(a.shape[1] // HD):
            squares += wide[:, j * HD : (j + 1) * HD]
        square[here, :] = squares

    each_part(source, layout, blocks, acc.shape[0] // 2, body)
    if final:
        mean = jnp.sum(square[...], axis=1, keepdims=True) / HDIM
        scaled = acc[...] * lax.rsqrt(mean + epsilon)
        out_ref[...] = (residual_ref[...].astype(jnp.float32) + scaled).astype(out_ref.dtype)


def project(source, inverse, weights, gathered, residual):
    rows, columns = residual.shape
    sums = [
        jax.ShapeDtypeStruct((rows, columns), jnp.float32),
        jax.ShapeDtypeStruct((rows, HD), jnp.float32),
    ]
    smem, vmem = pl.BlockSpec(memory_space=pltpu.SMEM), pl.BlockSpec(memory_space=pltpu.VMEM)
    arrays, layout = listed(gathered, [0, 1, 2])
    acc, square = pl.pallas_call(
        functools.partial(project_kernel, layout, False),
        in_specs=[smem] + [vmem] * (6 + len(arrays)),
        out_specs=[vmem] * 2,
        out_shape=sums,
        compiler_params=pltpu.CompilerParams(vmem_limit_bytes=18 * MIB),
    )(source, inverse, *weights, *arrays)
    arrays, layout = listed(gathered, [3])
    return pl.pallas_call(
        functools.partial(project_kernel, layout, True),
        in_specs=[smem] + [vmem] * (6 + len(arrays) + 3),
        out_specs=vmem,
        out_shape=jax.ShapeDtypeStruct((rows, columns), jnp.bfloat16),
        scratch_shapes=[pltpu.VMEM(x.shape, x.dtype) for x in sums],
        compiler_params=pltpu.CompilerParams(vmem_limit_bytes=18 * MIB),
    )(source, inverse, *weights, *arrays, acc, square, residual)


def encode_kernel(layout, late, first, final, *refs):
    source, *encoders = refs[: 3 if first else 4]
    used = 1 + len(encoders)
    blocks = refs[used : used + len(layout)]
    rest = refs[used + len(layout) :]
    if final:
        acc_ref, bias_ref, out_ref, acc = rest
    elif first:
        (acc,) = rest
    else:
        acc_ref, acc = rest
    if first:
        acc[...] = jnp.zeros_like(acc)
    else:
        acc[...] = acc_ref[...]
    depth = blocks[0].shape[1]

    def body(here, part, a, step):
        columns = pl.ds(pl.multiple_of(part * depth, BLK), depth)
        start = 0
        for n, e in enumerate(encoders):
            there = slice(start, start + e.shape[1])
            if step not in late or n == 2:
                acc[here, there] += dot(a, e[columns, :])
            start += e.shape[1]

    each_part(source, layout, blocks, acc.shape[0] // 2, body)
    if final:
        for i in range(out_ref.shape[0] // 8):
            pools = []
            for j in range(8 * i, 8 * i + 8):
                latent = jnp.maximum(acc[j * POOL : (j + 1) * POOL, :] + bias_ref[...], 0.0)
                pools.append(jnp.sum(latent, axis=0, keepdims=True) * (1.0 / POOL))
            out_ref[8 * i : 8 * i + 8, :] = jnp.concatenate(pools, axis=0)


def encode_own(source, encoders, gathered, bias):
    rows = gathered[0][0][0].shape[0] // 2
    smem, vmem = pl.BlockSpec(memory_space=pltpu.SMEM), pl.BlockSpec(memory_space=pltpu.VMEM)
    arrays, layout = listed(gathered, [0])
    return pl.pallas_call(
        functools.partial(encode_kernel, layout, (), True, False),
        in_specs=[smem] + [vmem] * (2 + len(arrays)),
        out_specs=vmem,
        out_shape=jax.ShapeDtypeStruct((rows, bias.shape[1]), jnp.float32),
        compiler_params=pltpu.CompilerParams(vmem_limit_bytes=30 * MIB),
    )(source, *encoders[:2], *arrays)


def encode(source, encoders, gathered, acc, bias):
    smem, vmem = pl.BlockSpec(memory_space=pltpu.SMEM), pl.BlockSpec(memory_space=pltpu.VMEM)
    params = pltpu.CompilerParams(vmem_limit_bytes=30 * MIB)
    shape = jax.ShapeDtypeStruct(acc.shape, acc.dtype)
    arrays, layout = listed(gathered, [0, 1, 2])
    acc = pl.pallas_call(
        functools.partial(encode_kernel, layout, (0,), False, False),
        in_specs=[smem] + [vmem] * (3 + len(arrays) + 1),
        out_specs=vmem,
        out_shape=shape,
        compiler_params=params,
    )(source, *encoders, *arrays, acc)
    arrays, layout = listed(gathered, [3])
    return pl.pallas_call(
        functools.partial(encode_kernel, layout, (), False, True),
        in_specs=[smem] + [vmem] * (3 + len(arrays) + 2),
        out_specs=vmem,
        out_shape=jax.ShapeDtypeStruct((acc.shape[0] // POOL, acc.shape[1]), jnp.float32),
        scratch_shapes=[pltpu.VMEM(acc.shape, acc.dtype)],
        compiler_params=params,
    )(source, *encoders, *arrays, acc, bias)


SIDE = 4
AXES = (("y", "z"), ("z", "y"))
HOPS = (0, 1, -1, 2)


def moved(x, axis, by):
    pairs = []
    for z in range(SIDE):
        for y in range(SIDE):
            to = (z, (y + by) % SIDE) if axis == "y" else ((z + by) % SIDE, y)
            pairs.append((z * SIDE + y, to[0] * SIDE + to[1]))
    return lax.ppermute(x, "seq", pairs)


def sources(place):
    z, y = place // SIDE, place % SIDE
    table = []
    for axis, _ in AXES:
        for second in HOPS:
            for first in HOPS:
                back_y, back_z = (first, second) if axis == "y" else (second, first)
                table.append((z - back_z) % SIDE * SIDE + (y - back_y) % SIDE)
    return jnp.stack(table).astype(jnp.int32)


def lines(halves):
    return [[half] + [moved(half, axis, by) for by in HOPS[1:]] for half, (axis, _) in zip(halves, AXES)]


def near(joined):
    return [(moved(x, axis, 1), moved(x, axis, -1)) for x, (_, axis) in zip(joined, AXES)]


def planes(joined, beside):
    out = []
    for x, (up, down), (_, axis) in zip(joined, beside, AXES):
        middle = x.shape[0] // 2
        across = (moved(up[:middle], axis, 1), moved(down[middle:], axis, -1))
        out.append(((x,), (up,), (down,), across))
    return out


def local(
    query_vectors,
    key_vectors,
    value_vectors,
    prior_state,
    doc_ids,
    norm_gain,
    residual,
    out_weight,
    enc_weight,
    enc_bias,
):
    groups, sections = lax.axis_size("head"), lax.axis_size("section")
    group, place = lax.axis_index("head"), lax.axis_index("seq")

    def from_head(x, by):
        return lax.ppermute(x, "head", [((i + by) % groups, i) for i in range(groups)])

    def from_section(x, by):
        pairs = []
        for s in range(sections):
            for i in range(groups):
                target = (s + 1) % sections
                pairs.append((s * groups + (i + by) % groups, target * groups + i))
        return lax.ppermute(x, ("section", "head"), pairs)

    packed = pack(query_vectors[0], key_vectors[0], value_vectors[0], doc_ids)
    weight = out_weight[0]
    middle = weight.shape[0] // 2
    after_upper, before_lower = from_head(weight[:middle], 1), from_head(weight[middle:], -1)
    after_upper, before_lower, rest = lax.optimization_barrier((after_upper, before_lower, weight))
    across = [from_head(after_upper, 1), from_head(before_lower, -1)]
    after_lower, before_upper = from_head(rest[middle:], 1), from_head(rest[:middle], -1)
    gains = [norm_gain] + [from_head(norm_gain, k) for k in range(1, groups)]
    inverse = jnp.concatenate([(1.0 / (g * g)).reshape(-1, HD) for g in gains], axis=1)
    half = enc_weight.shape[2] // 2
    bias = jnp.concatenate(
        [enc_bias, from_head(enc_bias[:, :half], -1), from_head(enc_bias[:, half:], 1)], axis=1
    )
    source = sources(place)

    packed = lax.all_to_all(packed, "seq", 0, 0, tiled=True)
    prior = lax.dynamic_index_in_dim(prior_state[0], place, 0, False)
    gain = lax.dynamic_slice_in_dim(norm_gain, place * HD, HD, 1)
    attended = attend(packed, prior, gain, groups)
    attended, after_lower, before_upper, inverse, bias = lax.optimization_barrier(
        (attended, after_lower, before_upper, inverse, bias)
    )

    own = lax.all_to_all(attended, "head", 0, 0, tiled=True)
    own = jnp.concatenate(
        [
            lax.dynamic_index_in_dim(own, (group + k) % groups, 0, False)
            for k in range(groups)
        ],
        axis=1,
    )
    own, across, first_half = lax.optimization_barrier((own, across, enc_weight[0][:, :half]))
    from_before = from_head(first_half, -1)
    rows = own.shape[0] // 2
    joined = [jnp.concatenate(line, axis=0) for line in lines([own[:rows], own[rows:]])]
    weights = [
        weight,
        jnp.concatenate([after_upper, after_lower], axis=0),
        *across,
        jnp.concatenate([before_upper, before_lower], axis=0),
    ]
    layer_out = project(source, inverse, weights, planes(joined, near(joined)), residual[0])

    layer_out, from_before, second_half = lax.optimization_barrier(
        (layer_out, from_before, enc_weight[0][:, half:])
    )
    from_after = from_head(second_half, 1)
    opposite = from_head(layer_out, 2)
    joined = [jnp.concatenate(line, axis=0) for line in lines([layer_out, opposite])]
    beside = near(joined)
    encoders = [enc_weight[0], from_before, from_after]
    acc = encode_own(source, encoders, [((x,),) for x in joined], bias)
    beside, acc = lax.optimization_barrier((beside, acc))
    pooled = encode(source, encoders, planes(joined, beside), acc, bias)
    pooled = pooled.astype(jnp.bfloat16)
    pools = pooled.shape[0] // 2
    mine = from_section(pooled[:, : 2 * half], 0)
    after = from_section(pooled[:, 2 * half : 3 * half], 1)
    before = from_section(pooled[:, 3 * half :], -1)
    turned = [
        mine[:pools],
        jnp.concatenate([after[:pools], before[pools:]], axis=1),
        mine[pools:],
        jnp.concatenate([after[pools:], before[:pools]], axis=1),
    ]
    turned = jnp.stack(turned)
    monitor = jnp.concatenate(
        [
            lax.dynamic_index_in_dim(turned, (i - group) % groups, 0, False)
            for i in range(groups)
        ],
        axis=0,
    )
    return (from_section(layer_out[None], 0), monitor[None])


def solution(mesh):
    return jax.shard_map(
        local,
        mesh=mesh,
        in_specs=(
            P("section", "seq", "head"),
            P("section", "seq", "head"),
            P("section", "seq", "head"),
            P("section", "head", None, None),
            P("section", "seq"),
            P("section", "head"),
            P("section", "head", "seq"),
            P("section", "head", "seq"),
            P("section", None, ("seq", "head")),
            P("section", ("seq", "head")),
        ),
        out_specs=(P("section", "head", "seq"), P("section", None, ("seq", "head"))),
        check_vma=False,
    )
```

```python
import functools

import jax
import jax.numpy as jnp
from jax import lax
from jax.experimental import pallas as pl
from jax.experimental.pallas import tpu as pltpu
from jax.sharding import PartitionSpec as P

HD = 128
POOL = 64
HDIM = 8192
BLK = 128
PACK = 3 * BLK + 16

epsilon = 1e-06
MIB = 1 << 20


def dot(a, b, dims=((1,), (0,))):
    return lax.dot_general(a, b, (dims, ((), ())), preferred_element_type=jnp.float32)


def split(x):
    high = x.astype(jnp.bfloat16)
    return high, (x - high.astype(jnp.float32)).astype(jnp.bfloat16)


def in_hbm(x):
    return pltpu.with_memory_space_constraint(x, pltpu.HBM)


def pack_kernel(queries_ref, keys_ref, values_ref, docs_ref, out_ref):
    docs = jnp.broadcast_to(docs_ref[...].astype(jnp.float32), (PACK - 3 * BLK, BLK))
    docs = docs.astype(out_ref.dtype)
    for head in range(out_ref.shape[0]):
        columns = slice(head * HD, (head + 1) * HD)
        out_ref[head, 0:BLK, :] = queries_ref[:, columns]
        out_ref[head, BLK : 2 * BLK, :] = keys_ref[:, columns]
        out_ref[head, 2 * BLK : 3 * BLK, :] = values_ref[:, columns]
        out_ref[head, 3 * BLK : PACK, :] = docs


def pack(queries, keys, values, docs):
    heads = queries.shape[1] // HD
    return pl.pallas_call(
        pack_kernel,
        out_shape=jax.ShapeDtypeStruct((heads, PACK, HD), jnp.bfloat16),
        compiler_params=pltpu.CompilerParams(vmem_limit_bytes=12 * MIB),
    )(*[in_hbm(x) for x in (queries, keys, values)], docs)


def attend_kernel(packed_ref, prior_ref, gain_ref, out_ref):
    groups, per_group = out_ref.shape[0], packed_ref.shape[0] // out_ref.shape[0]
    row = lax.broadcasted_iota(jnp.int32, (BLK, BLK), 0)
    col = lax.broadcasted_iota(jnp.int32, (BLK, BLK), 1)
    causal = col <= row
    gain = gain_ref[...]
    state = prior_ref[...]
    last = jnp.zeros((BLK, BLK), jnp.float32)
    for group in range(groups):
        for member in range(per_group):
            block = group * per_group + member
            queries = packed_ref[block, 0:BLK, :]
            keys = packed_ref[block, BLK : 2 * BLK, :]
            values = packed_ref[block, 2 * BLK : 3 * BLK, :]
            along = jnp.broadcast_to(
                packed_ref[block, 3 * BLK : PACK, :].astype(jnp.float32)[0:1, :], (BLK, BLK)
            )
            down = along.T
            scores = dot(queries, keys, ((1,), (1,)))
            scores = jnp.where(causal & (along == down), scores, 0.0)
            high, low = split(scores)
            intra = dot(high, values) + dot(low, values)
            high, low = split(state)
            inter = dot(queries, high) + dot(queries, low)
            attended = jnp.where(down == last, inter, 0.0) + intra
            rows = slice(member * BLK, (member + 1) * BLK)
            out_ref[group, rows, :] = (attended * gain).astype(out_ref.dtype)
            newest = jnp.broadcast_to(along[:, BLK - 1 :], (BLK, BLK))
            chosen = jnp.where(down == newest, keys.astype(jnp.float32), 0.0)
            summary = dot(chosen.astype(jnp.bfloat16), values, ((0,), (0,)))
            state = jnp.where(last == newest, state, 0.0) + summary
            last = newest


def attend(packed, prior, gain, groups):
    rows = packed.shape[0] * BLK // groups
    return pl.pallas_call(
        attend_kernel,
        out_shape=jax.ShapeDtypeStruct((groups, rows, HD), jnp.bfloat16),
        compiler_params=pltpu.CompilerParams(vmem_limit_bytes=12 * MIB),
    )(packed, prior, gain)


def listed(gathered, steps):
    return [array for step in steps for parts in gathered for array in parts[step]]


def stream(source, step, arrays, rows, buffer, sems, fetch, fetched, body):
    total = sum(array.shape[0] // rows for array in arrays)
    count = total // len(arrays)

    def place(n):
        half = lax.rem(lax.div(n, 4), 2)
        row = half * 4 + step + lax.div(n, 8)
        return half, source[row * 4 + lax.rem(n, 4)]

    def start(n, slot):
        for r, array in enumerate(arrays):

            @pl.when(lax.div(n, count) == r)
            def _():
                across = pl.ds(pl.multiple_of(lax.rem(n, count) * rows, BLK), rows)
                pltpu.make_async_copy(array.at[across, :], buffer.at[slot], sems.at[slot, 0]).start()

        fetch(place(n)[1], slot)

    start(0, 0)

    def one(n, carry):
        slot = lax.rem(n, 2)

        @pl.when(n + 1 < total)
        def _():
            start(n + 1, 1 - slot)

        first = pl.ds(0, rows)
        pltpu.make_async_copy(arrays[0].at[first, :], buffer.at[slot], sems.at[slot, 0]).wait()
        half, part = place(n)
        fetched(slot)
        body(pl.ds(pl.multiple_of(half * rows, BLK), rows), part, slot)
        return carry

    lax.fori_loop(0, total, one, 0)


def project_kernel(count, step, final, *refs):
    source, inverse_ref, w0, w1, w2, w3, w4 = refs[:7]
    blocks = refs[7 : 7 + count]
    *rest, buffer, w_buffer, sems = refs[7 + count :]
    if final:
        acc_ref, square_ref, residual_ref, out_ref, acc, square = rest
        acc[...] = acc_ref[...]
        square[...] = square_ref[...]
    else:
        acc, square = rest
        acc[...] = jnp.zeros_like(acc)
        square[...] = jnp.zeros_like(square)
    middle = w2.shape[0] // HD

    def copy(ref, block, k, slot):
        rows = pl.ds(pl.multiple_of(block * HD, HD), HD)
        there = w_buffer.at[slot, k * HD : (k + 1) * HD, :]
        return pltpu.make_async_copy(ref.at[rows, :], there, sems.at[slot, 1 + k])

    def fetch(part, slot):
        for k, w in ((0, w0), (1, w1), (3, w4)):
            copy(w, part, k, slot).start()

        @pl.when(part < middle)
        def _():
            copy(w2, part, 2, slot).start()

        @pl.when(part >= middle)
        def _():
            copy(w3, part - middle, 2, slot).start()

    def fetched(slot):
        for k in range(4):
            copy(w0, 0, k, slot).wait()

    def body(here, part, slot):
        a = buffer[slot]
        acc[here, :] += dot(a, w_buffer[slot])
        wide = a.astype(jnp.float32)
        wide = wide * wide * inverse_ref[pl.ds(part, 1), :]
        squares = square[here, :]
        for j in range(a.shape[1] // HD):
            squares += wide[:, j * HD : (j + 1) * HD]
        square[here, :] = squares

    stream(source, step, blocks, buffer.shape[1], buffer, sems, fetch, fetched, body)
    if final:
        mean = jnp.sum(square[...], axis=1, keepdims=True) / HDIM
        scaled = acc[...] * lax.rsqrt(mean + epsilon)
        out_ref[...] = (residual_ref[...].astype(jnp.float32) + scaled).astype(out_ref.dtype)


SMEM, VMEM, HBM, ANY = (
    pl.BlockSpec(memory_space=x) for x in (pltpu.SMEM, pltpu.VMEM, pltpu.HBM, pl.ANY)
)


def project(source, inverse, weights, gathered, residual):
    rows, columns = residual.shape
    depth = gathered[0][0][0].shape[1]
    sums = [
        jax.ShapeDtypeStruct((rows, columns), jnp.float32),
        jax.ShapeDtypeStruct((rows, HD), jnp.float32),
    ]
    slots = [
        pltpu.VMEM((2, rows // 2, depth), jnp.bfloat16),
        pltpu.VMEM((2, depth, columns), jnp.bfloat16),
        pltpu.SemaphoreType.DMA((2, 5)),
    ]
    params = pltpu.CompilerParams(vmem_limit_bytes=12 * MIB)
    weights = [in_hbm(w) for w in weights]
    arrays = listed(gathered, [0, 1, 2])
    acc, square = pl.pallas_call(
        functools.partial(project_kernel, len(arrays), 0, False),
        in_specs=[SMEM, VMEM] + [HBM] * 5 + [ANY] * len(arrays),
        out_specs=[VMEM] * 2,
        out_shape=sums,
        scratch_shapes=slots,
        compiler_params=params,
    )(source, inverse, *weights, *arrays)
    arrays = listed(gathered, [3])
    return pl.pallas_call(
        functools.partial(project_kernel, len(arrays), 3, True),
        in_specs=[SMEM, VMEM] + [HBM] * 5 + [ANY] * len(arrays) + [VMEM] * 3,
        out_specs=VMEM,
        out_shape=jax.ShapeDtypeStruct((rows, columns), jnp.bfloat16),
        scratch_shapes=[pltpu.VMEM(x.shape, x.dtype) for x in sums] + slots,
        compiler_params=params,
    )(source, inverse, *weights, *arrays, acc, square, residual)


def encode_kernel(encoder_count, count, step, late, final, *refs):
    source, *encoders = refs[: 1 + encoder_count]
    blocks = refs[1 + encoder_count : 1 + encoder_count + count]
    *rest, buffer, e_buffer, sems = refs[1 + encoder_count + count :]
    if final:
        acc_ref, bias_ref, out_ref, acc = rest
    elif encoder_count == 2:
        (acc,) = rest
        acc_ref = None
    else:
        acc_ref, acc = rest
    acc[...] = jnp.zeros_like(acc) if acc_ref is None else acc_ref[...]
    depth = e_buffer.shape[1]
    starts = [sum(e.shape[1] for e in encoders[:n]) for n in range(encoder_count)]

    def run(step, blocks, used):
        def there(n):
            return slice(starts[n], starts[n] + encoders[n].shape[1])

        def copy(n, part, slot):
            rows = pl.ds(pl.multiple_of(part * depth, BLK), depth)
            to = e_buffer.at[slot, :, there(n)]
            return pltpu.make_async_copy(encoders[n].at[rows, :], to, sems.at[slot, 1 + n])

        def fetch(part, slot):
            for n in used:
                copy(n, part, slot).start()

        def fetched(slot):
            for n in used:
                copy(n, 0, slot).wait()

        def body(here, part, slot):
            across = slice(starts[used[0]], there(used[-1]).stop)
            acc[here, across] += dot(buffer[slot], e_buffer[slot, :, across])

        stream(source, step, blocks, buffer.shape[1], buffer, sems, fetch, fetched, body)

    every = list(range(encoder_count))
    if late:
        run(step, blocks[:late], every[-1:])
        run(step + 1, blocks[late:], every)
    else:
        run(step, blocks, every)
    if final:
        for i in range(out_ref.shape[0] // 8):
            pools = []
            for j in range(8 * i, 8 * i + 8):
                latent = jnp.maximum(acc[j * POOL : (j + 1) * POOL, :] + bias_ref[...], 0.0)
                pools.append(jnp.sum(latent, axis=0, keepdims=True) * (1.0 / POOL))
            out_ref[8 * i : 8 * i + 8, :] = jnp.concatenate(pools, axis=0)


def encode(source, encoders, arrays, step, late=0, acc=None, bias=None):
    rows, depth = arrays[0].shape[0] // (4 if bias is None else 2), arrays[0].shape[1]
    width = 4 * encoders[1].shape[1]
    shape = jax.ShapeDtypeStruct((2 * rows, width), jnp.float32)
    final = bias is not None
    extra = [x for x in (acc, bias) if x is not None]
    slots = [
        pltpu.VMEM((2, rows, depth), jnp.bfloat16),
        pltpu.VMEM((2, depth, width), jnp.bfloat16),
        pltpu.SemaphoreType.DMA((2, 4)),
    ]
    return pl.pallas_call(
        functools.partial(encode_kernel, len(encoders), len(arrays), step, late, final),
        in_specs=[SMEM] + [HBM] * len(encoders) + [ANY] * len(arrays) + [VMEM] * len(extra),
        out_specs=VMEM,
        out_shape=jax.ShapeDtypeStruct((2 * rows // POOL, width), jnp.float32) if final else shape,
        scratch_shapes=([pltpu.VMEM(shape.shape, shape.dtype)] if final else []) + slots,
        compiler_params=pltpu.CompilerParams(vmem_limit_bytes=18 * MIB),
    )(source, *[in_hbm(x) for x in encoders], *arrays, *extra)


SIDE = 4
AXES = (("y", "z"), ("z", "y"))
HOPS = (0, 1, -1, 2)


def moved(x, axis, by):
    pairs = []
    for z in range(SIDE):
        for y in range(SIDE):
            to = (z, (y + by) % SIDE) if axis == "y" else ((z + by) % SIDE, y)
            pairs.append((z * SIDE + y, to[0] * SIDE + to[1]))
    return lax.ppermute(x, "seq", pairs)


def sources(place):
    z, y = place // SIDE, place % SIDE
    table = []
    for axis, _ in AXES:
        for second in HOPS:
            for first in HOPS:
                back_y, back_z = (first, second) if axis == "y" else (second, first)
                table.append((z - back_z) % SIDE * SIDE + (y - back_y) % SIDE)
    return jnp.stack(table).astype(jnp.int32)


def lines(halves):
    return [[half] + [moved(half, axis, by) for by in HOPS[1:]] for half, (axis, _) in zip(halves, AXES)]


def near(joined):
    return [(moved(x, axis, 1), moved(x, axis, -1)) for x, (_, axis) in zip(joined, AXES)]


def planes(joined, beside):
    out = []
    for x, (up, down), (_, axis) in zip(joined, beside, AXES):
        middle = x.shape[0] // 2
        across = (moved(up[:middle], axis, 1), moved(down[middle:], axis, -1))
        out.append(((x,), (up,), (down,), across))
    return out


def local(
    query_vectors,
    key_vectors,
    value_vectors,
    prior_state,
    doc_ids,
    norm_gain,
    residual,
    out_weight,
    enc_weight,
    enc_bias,
):
    groups, sections = lax.axis_size("head"), lax.axis_size("section")
    group, place = lax.axis_index("head"), lax.axis_index("seq")

    def from_head(x, by):
        return lax.ppermute(x, "head", [((i + by) % groups, i) for i in range(groups)])

    def from_section(x, by):
        pairs = []
        for s in range(sections):
            for i in range(groups):
                target = (s + 1) % sections
                pairs.append((s * groups + (i + by) % groups, target * groups + i))
        return lax.ppermute(x, ("section", "head"), pairs)

    packed = pack(query_vectors[0], key_vectors[0], value_vectors[0], doc_ids)
    weight = out_weight[0]
    middle = weight.shape[0] // 2
    after, before = from_head(weight, 1), from_head(weight, -1)
    gains = [norm_gain] + [from_head(norm_gain, k) for k in range(1, groups)]
    inverse = jnp.concatenate([(1.0 / (g * g)).reshape(-1, HD) for g in gains], axis=1)
    half = enc_weight.shape[2] // 2
    bias = jnp.concatenate(
        [enc_bias, from_head(enc_bias[:, :half], -1), from_head(enc_bias[:, half:], 1)], axis=1
    )
    source = sources(place)

    packed = lax.all_to_all(packed, "seq", 0, 0, tiled=True)
    prior = lax.dynamic_index_in_dim(prior_state[0], place, 0, False)
    gain = lax.dynamic_slice_in_dim(norm_gain, place * HD, HD, 1)
    attended = attend(packed, prior, gain, groups)
    attended, after, before, inverse, bias = lax.optimization_barrier(
        (attended, after, before, inverse, bias)
    )
    across = [from_head(after[:middle], 1), from_head(before[middle:], -1)]

    own = lax.all_to_all(attended, "head", 0, 0, tiled=True)
    own = jnp.concatenate(
        [
            lax.dynamic_index_in_dim(own, (group + k) % groups, 0, False)
            for k in range(groups)
        ],
        axis=1,
    )
    own, across, first_half = lax.optimization_barrier((own, across, enc_weight[0][:, :half]))
    from_before = from_head(first_half, -1)
    rows = own.shape[0] // 2
    joined = [jnp.concatenate(line, axis=0) for line in lines([own[:rows], own[rows:]])]
    weights = [weight, after, *across, before]
    layer_out = project(source, inverse, weights, planes(joined, near(joined)), residual[0])

    layer_out, from_before, second_half = lax.optimization_barrier(
        (layer_out, from_before, enc_weight[0][:, half:])
    )
    from_after = from_head(second_half, 1)
    opposite = from_head(layer_out, 2)
    joined = [jnp.concatenate(line, axis=0) for line in lines([layer_out, opposite])]
    beside = near(joined)
    encoders = [enc_weight[0], from_before, from_after]
    acc = encode(source, encoders[:2], joined, 0)
    beside, acc = lax.optimization_barrier((beside, acc))
    gathered = planes(joined, beside)
    acc = encode(source, encoders, listed(gathered, [0, 1, 2]), 0, late=2, acc=acc)
    acc, layer_out = lax.optimization_barrier((acc, layer_out))
    pooled = encode(source, encoders, listed(gathered, [3]), 3, acc=acc, bias=bias)
    pooled = pooled.astype(jnp.bfloat16)
    pools = pooled.shape[0] // 2
    mine = from_section(pooled[:, : 2 * half], 0)
    after = from_section(pooled[:, 2 * half : 3 * half], 1)
    before = from_section(pooled[:, 3 * half :], -1)
    turned = [
        mine[:pools],
        jnp.concatenate([after[:pools], before[pools:]], axis=1),
        mine[pools:],
        jnp.concatenate([after[pools:], before[:pools]], axis=1),
    ]
    turned = jnp.stack(turned)
    monitor = jnp.concatenate(
        [
            lax.dynamic_index_in_dim(turned, (i - group) % groups, 0, False)
            for i in range(groups)
        ],
        axis=0,
    )
    return (from_section(layer_out[None], 0), monitor[None])


def solution(mesh):
    return jax.shard_map(
        local,
        mesh=mesh,
        in_specs=(
            P("section", "seq", "head"),
            P("section", "seq", "head"),
            P("section", "seq", "head"),
            P("section", "head", None, None),
            P("section", "seq"),
            P("section", "head"),
            P("section", "head", "seq"),
            P("section", "head", "seq"),
            P("section", None, ("seq", "head")),
            P("section", ("seq", "head")),
        ),
        out_specs=(P("section", "head", "seq"), P("section", None, ("seq", "head"))),
        check_vma=False,
    )
```

```python
import functools

import jax
import jax.numpy as jnp
from jax import lax
from jax.experimental import pallas as pl
from jax.experimental.pallas import tpu as pltpu
from jax.sharding import PartitionSpec as P

HD = 128
POOL = 64
HDIM = 8192
BLK = 128
PACK = 3 * BLK + 16

epsilon = 1e-06
MIB = 1 << 20


def dot(a, b, dims=((1,), (0,))):
    return lax.dot_general(a, b, (dims, ((), ())), preferred_element_type=jnp.float32)


def split(x):
    high = x.astype(jnp.bfloat16)
    return high, (x - high.astype(jnp.float32)).astype(jnp.bfloat16)


def in_hbm(x):
    return pltpu.with_memory_space_constraint(x, pltpu.HBM)


def pack_kernel(queries_ref, keys_ref, values_ref, docs_ref, out_ref):
    docs = jnp.broadcast_to(docs_ref[...].astype(jnp.float32), (PACK - 3 * BLK, BLK))
    docs = docs.astype(out_ref.dtype)
    for head in range(out_ref.shape[0]):
        columns = slice(head * HD, (head + 1) * HD)
        out_ref[head, 0:BLK, :] = queries_ref[:, columns]
        out_ref[head, BLK : 2 * BLK, :] = keys_ref[:, columns]
        out_ref[head, 2 * BLK : 3 * BLK, :] = values_ref[:, columns]
        out_ref[head, 3 * BLK : PACK, :] = docs


def pack(queries, keys, values, docs):
    heads = queries.shape[1] // HD
    return pl.pallas_call(
        pack_kernel,
        out_shape=jax.ShapeDtypeStruct((heads, PACK, HD), jnp.bfloat16),
        compiler_params=pltpu.CompilerParams(vmem_limit_bytes=12 * MIB),
    )(*[in_hbm(x) for x in (queries, keys, values)], docs)


def attend_kernel(packed_ref, prior_ref, gain_ref, out_ref):
    groups, per_group = out_ref.shape[0], packed_ref.shape[0] // out_ref.shape[0]
    row = lax.broadcasted_iota(jnp.int32, (BLK, BLK), 0)
    col = lax.broadcasted_iota(jnp.int32, (BLK, BLK), 1)
    causal = col <= row
    gain = gain_ref[...]
    state = prior_ref[...]
    last = jnp.zeros((BLK, BLK), jnp.float32)
    for group in range(groups):
        for member in range(per_group):
            block = group * per_group + member
            queries = packed_ref[block, 0:BLK, :]
            keys = packed_ref[block, BLK : 2 * BLK, :]
            values = packed_ref[block, 2 * BLK : 3 * BLK, :]
            along = jnp.broadcast_to(
                packed_ref[block, 3 * BLK : PACK, :].astype(jnp.float32)[0:1, :], (BLK, BLK)
            )
            down = along.T
            scores = dot(queries, keys, ((1,), (1,)))
            scores = jnp.where(causal & (along == down), scores, 0.0)
            high, low = split(scores)
            intra = dot(high, values) + dot(low, values)
            high, low = split(state)
            inter = dot(queries, high) + dot(queries, low)
            attended = jnp.where(down == last, inter, 0.0) + intra
            rows = slice(member * BLK, (member + 1) * BLK)
            out_ref[group, rows, :] = (attended * gain).astype(out_ref.dtype)
            newest = jnp.broadcast_to(along[:, BLK - 1 :], (BLK, BLK))
            chosen = jnp.where(down == newest, keys.astype(jnp.float32), 0.0)
            summary = dot(chosen.astype(jnp.bfloat16), values, ((0,), (0,)))
            state = jnp.where(last == newest, state, 0.0) + summary
            last = newest


def attend(packed, prior, gain, groups):
    rows = packed.shape[0] * BLK // groups
    return pl.pallas_call(
        attend_kernel,
        out_shape=jax.ShapeDtypeStruct((groups, rows, HD), jnp.bfloat16),
        compiler_params=pltpu.CompilerParams(vmem_limit_bytes=12 * MIB),
    )(packed, prior, gain)


SLOTS = 4


def listed(gathered, steps):
    return [array for step in steps for parts in gathered for array in parts[step]]


def stream(source, step, arrays, rows, buffer, sems, fetch, fetched, body):
    total = sum(array.shape[0] // rows for array in arrays)
    count = total // len(arrays)

    def place(n):
        half = lax.rem(lax.div(n, 4), 2)
        row = half * 4 + step + lax.div(n, 8)
        return half, source[row * 4 + lax.rem(n, 4)]

    def start(n, slot):
        for r, array in enumerate(arrays):

            @pl.when(lax.div(n, count) == r)
            def _():
                across = pl.ds(pl.multiple_of(lax.rem(n, count) * rows, BLK), rows)
                pltpu.make_async_copy(array.at[across, :], buffer.at[slot], sems.at[slot, 0]).start()

        fetch(place(n)[1], slot)

    for n in range(SLOTS - 1):
        start(n, n)

    def one(n, carry):
        slot = lax.rem(n, SLOTS)

        @pl.when(n + SLOTS - 1 < total)
        def _():
            start(n + SLOTS - 1, lax.rem(n + SLOTS - 1, SLOTS))

        first = pl.ds(0, rows)
        pltpu.make_async_copy(arrays[0].at[first, :], buffer.at[slot], sems.at[slot, 0]).wait()
        half, part = place(n)
        fetched(slot)
        body(pl.ds(pl.multiple_of(half * rows, BLK), rows), part, slot)
        return carry

    lax.fori_loop(0, total, one, 0)


def project_kernel(count, step, final, *refs):
    source, inverse_ref, w0, w1, w2, w3, w4 = refs[:7]
    blocks = refs[7 : 7 + count]
    *rest, buffer, w_buffer, sems = refs[7 + count :]
    if final:
        acc_ref, square_ref, residual_ref, out_ref, acc, square = rest
        acc[...] = acc_ref[...]
        square[...] = square_ref[...]
    else:
        acc, square = rest
        acc[...] = jnp.zeros_like(acc)
        square[...] = jnp.zeros_like(square)
    middle = w2.shape[0] // HD

    def copy(ref, block, k, slot):
        rows = pl.ds(pl.multiple_of(block * HD, HD), HD)
        there = w_buffer.at[slot, k * HD : (k + 1) * HD, :]
        return pltpu.make_async_copy(ref.at[rows, :], there, sems.at[slot, 1 + k])

    def fetch(part, slot):
        for k, w in ((0, w0), (1, w1), (3, w4)):
            copy(w, part, k, slot).start()

        @pl.when(part < middle)
        def _():
            copy(w2, part, 2, slot).start()

        @pl.when(part >= middle)
        def _():
            copy(w3, part - middle, 2, slot).start()

    def fetched(slot):
        for k in range(4):
            copy(w0, 0, k, slot).wait()

    def body(here, part, slot):
        a = buffer[slot]
        acc[here, :] += dot(a, w_buffer[slot])
        wide = a.astype(jnp.float32)
        wide = wide * wide * inverse_ref[pl.ds(part, 1), :]
        squares = square[here, :]
        for j in range(a.shape[1] // HD):
            squares += wide[:, j * HD : (j + 1) * HD]
        square[here, :] = squares

    stream(source, step, blocks, buffer.shape[1], buffer, sems, fetch, fetched, body)
    if final:
        mean = jnp.sum(square[...], axis=1, keepdims=True) / HDIM
        scaled = acc[...] * lax.rsqrt(mean + epsilon)
        out_ref[...] = (residual_ref[...].astype(jnp.float32) + scaled).astype(out_ref.dtype)


SMEM, VMEM, HBM, ANY = (
    pl.BlockSpec(memory_space=x) for x in (pltpu.SMEM, pltpu.VMEM, pltpu.HBM, pl.ANY)
)


def project(source, inverse, weights, gathered, residual):
    rows, columns = residual.shape
    depth = gathered[0][0][0].shape[1]
    sums = [
        jax.ShapeDtypeStruct((rows, columns), jnp.float32),
        jax.ShapeDtypeStruct((rows, HD), jnp.float32),
    ]
    slots = [
        pltpu.VMEM((SLOTS, rows // 2, depth), jnp.bfloat16),
        pltpu.VMEM((SLOTS, depth, columns), jnp.bfloat16),
        pltpu.SemaphoreType.DMA((SLOTS, 5)),
    ]
    params = pltpu.CompilerParams(vmem_limit_bytes=12 * MIB)
    weights = [in_hbm(w) for w in weights]
    arrays = listed(gathered, [0, 1, 2])
    acc, square = pl.pallas_call(
        functools.partial(project_kernel, len(arrays), 0, False),
        in_specs=[SMEM, VMEM] + [HBM] * 5 + [ANY] * len(arrays),
        out_specs=[VMEM] * 2,
        out_shape=sums,
        scratch_shapes=slots,
        compiler_params=params,
    )(source, inverse, *weights, *arrays)
    arrays = listed(gathered, [3])
    return pl.pallas_call(
        functools.partial(project_kernel, len(arrays), 3, True),
        in_specs=[SMEM, VMEM] + [HBM] * 5 + [ANY] * len(arrays) + [VMEM] * 3,
        out_specs=VMEM,
        out_shape=jax.ShapeDtypeStruct((rows, columns), jnp.bfloat16),
        scratch_shapes=[pltpu.VMEM(x.shape, x.dtype) for x in sums] + slots,
        compiler_params=params,
    )(source, inverse, *weights, *arrays, acc, square, residual)


def encode_kernel(encoder_count, count, step, late, final, *refs):
    source, *encoders = refs[: 1 + encoder_count]
    blocks = refs[1 + encoder_count : 1 + encoder_count + count]
    *rest, buffer, e_buffer, sems = refs[1 + encoder_count + count :]
    if final:
        acc_ref, bias_ref, out_ref, acc = rest
    elif encoder_count == 2:
        (acc,) = rest
        acc_ref = None
    else:
        acc_ref, acc = rest
    acc[...] = jnp.zeros_like(acc) if acc_ref is None else acc_ref[...]
    depth = e_buffer.shape[1]
    starts = [sum(e.shape[1] for e in encoders[:n]) for n in range(encoder_count)]

    def run(step, blocks, used):
        def there(n):
            return slice(starts[n], starts[n] + encoders[n].shape[1])

        def copy(n, part, slot):
            rows = pl.ds(pl.multiple_of(part * depth, BLK), depth)
            to = e_buffer.at[slot, :, there(n)]
            return pltpu.make_async_copy(encoders[n].at[rows, :], to, sems.at[slot, 1 + n])

        def fetch(part, slot):
            for n in used:
                copy(n, part, slot).start()

        def fetched(slot):
            for n in used:
                copy(n, 0, slot).wait()

        def body(here, part, slot):
            across = slice(starts[used[0]], there(used[-1]).stop)
            acc[here, across] += dot(buffer[slot], e_buffer[slot, :, across])

        stream(source, step, blocks, buffer.shape[1], buffer, sems, fetch, fetched, body)

    every = list(range(encoder_count))
    if late:
        run(step, blocks[:late], every[-1:])
        run(step + 1, blocks[late:], every)
    else:
        run(step, blocks, every)
    if final:
        for i in range(out_ref.shape[0] // 8):
            pools = []
            for j in range(8 * i, 8 * i + 8):
                latent = jnp.maximum(acc[j * POOL : (j + 1) * POOL, :] + bias_ref[...], 0.0)
                pools.append(jnp.sum(latent, axis=0, keepdims=True) * (1.0 / POOL))
            out_ref[8 * i : 8 * i + 8, :] = jnp.concatenate(pools, axis=0)


def encode(source, encoders, arrays, step, late=0, acc=None, bias=None):
    rows, depth = arrays[0].shape[0] // (4 if bias is None else 2), arrays[0].shape[1]
    width = 4 * encoders[1].shape[1]
    shape = jax.ShapeDtypeStruct((2 * rows, width), jnp.float32)
    final = bias is not None
    extra = [x for x in (acc, bias) if x is not None]
    slots = [
        pltpu.VMEM((SLOTS, rows, depth), jnp.bfloat16),
        pltpu.VMEM((SLOTS, depth, width), jnp.bfloat16),
        pltpu.SemaphoreType.DMA((SLOTS, 4)),
    ]
    return pl.pallas_call(
        functools.partial(encode_kernel, len(encoders), len(arrays), step, late, final),
        in_specs=[SMEM] + [HBM] * len(encoders) + [ANY] * len(arrays) + [VMEM] * len(extra),
        out_specs=VMEM,
        out_shape=jax.ShapeDtypeStruct((2 * rows // POOL, width), jnp.float32) if final else shape,
        scratch_shapes=([pltpu.VMEM(shape.shape, shape.dtype)] if final else []) + slots,
        compiler_params=pltpu.CompilerParams(vmem_limit_bytes=18 * MIB),
    )(source, *[in_hbm(x) for x in encoders], *arrays, *extra)


SIDE = 4
AXES = (("y", "z"), ("z", "y"))
HOPS = (0, 1, -1, 2)


def moved(x, axis, by):
    pairs = []
    for z in range(SIDE):
        for y in range(SIDE):
            to = (z, (y + by) % SIDE) if axis == "y" else ((z + by) % SIDE, y)
            pairs.append((z * SIDE + y, to[0] * SIDE + to[1]))
    return lax.ppermute(x, "seq", pairs)


def sources(place):
    z, y = place // SIDE, place % SIDE
    table = []
    for axis, _ in AXES:
        for second in HOPS:
            for first in HOPS:
                back_y, back_z = (first, second) if axis == "y" else (second, first)
                table.append((z - back_z) % SIDE * SIDE + (y - back_y) % SIDE)
    return jnp.stack(table).astype(jnp.int32)


def lines(halves):
    return [[half] + [moved(half, axis, by) for by in HOPS[1:]] for half, (axis, _) in zip(halves, AXES)]


def near(joined):
    return [(moved(x, axis, 1), moved(x, axis, -1)) for x, (_, axis) in zip(joined, AXES)]


def planes(joined, beside):
    out = []
    for x, (up, down), (_, axis) in zip(joined, beside, AXES):
        middle = x.shape[0] // 2
        across = (moved(up[:middle], axis, 1), moved(down[middle:], axis, -1))
        out.append(((x,), (up,), (down,), across))
    return out


def local(
    query_vectors,
    key_vectors,
    value_vectors,
    prior_state,
    doc_ids,
    norm_gain,
    residual,
    out_weight,
    enc_weight,
    enc_bias,
):
    groups, sections = lax.axis_size("head"), lax.axis_size("section")
    group, place = lax.axis_index("head"), lax.axis_index("seq")

    def from_head(x, by):
        return lax.ppermute(x, "head", [((i + by) % groups, i) for i in range(groups)])

    def paired(shift):
        pairs = [((i + shift) % groups, (i + 1 + shift) % groups) for i in range(0, groups, 2)]
        return [pair for a, b in pairs for pair in ((a, b), (b, a))]

    def from_section(x, pairs=None):
        both = []
        for s in range(sections):
            for a, b in pairs or [(i, i) for i in range(groups)]:
                both.append((s * groups + a, (s + 1) % sections * groups + b))
        return lax.ppermute(x, ("section", "head"), both)

    packed = pack(query_vectors[0], key_vectors[0], value_vectors[0], doc_ids)
    weight = out_weight[0]
    middle = weight.shape[0] // 2
    after, before = from_head(weight, 1), from_head(weight, -1)
    gains = [norm_gain] + [from_head(norm_gain, k) for k in range(1, groups)]
    inverse = jnp.concatenate([(1.0 / (g * g)).reshape(-1, HD) for g in gains], axis=1)
    half = enc_weight.shape[2] // 2
    odd = group % 2

    def halves(x):
        return [lax.dynamic_slice_in_dim(x, n * half, half, 1) for n in (odd, 1 - odd)]

    first_bias, second_bias = halves(enc_bias)
    bias = jnp.concatenate(
        [
            enc_bias,
            lax.ppermute(first_bias, "head", paired(0)),
            lax.ppermute(second_bias, "head", paired(1)),
        ],
        axis=1,
    )
    source = sources(place)

    packed = lax.all_to_all(packed, "seq", 0, 0, tiled=True)
    packed, after, before, inverse, bias = lax.optimization_barrier(
        (packed, after, before, inverse, bias)
    )
    prior = lax.dynamic_index_in_dim(prior_state[0], place, 0, False)
    gain = lax.dynamic_slice_in_dim(norm_gain, place * HD, HD, 1)
    attended = attend(packed, prior, gain, groups)

    own = lax.all_to_all(attended, "head", 0, 0, tiled=True)
    own = jnp.concatenate(
        [
            lax.dynamic_index_in_dim(own, (group + k) % groups, 0, False)
            for k in range(groups)
        ],
        axis=1,
    )
    own, *parts = lax.optimization_barrier((own, after[:middle], before[middle:]))
    across = [from_head(parts[0], 1), from_head(parts[1], -1)]
    rows = own.shape[0] // 2
    joined = [jnp.concatenate(line, axis=0) for line in lines([own[:rows], own[rows:]])]
    first, second = halves(enc_weight[0])
    _, across, first, second = lax.optimization_barrier((joined, across, first, second))
    first = lax.ppermute(first, "head", paired(0))
    second = lax.all_to_all(
        jnp.broadcast_to(second[None], (2, *second.shape)),
        "head",
        0,
        0,
        axis_index_groups=[[(i + 1) % groups, (i + 2) % groups] for i in range(0, groups, 2)],
        tiled=True,
    )
    second = lax.dynamic_index_in_dim(second, odd, 0, False)
    weights = [weight, after, *across, before]
    layer_out = project(source, inverse, weights, planes(joined, near(joined)), residual[0])
    opposite = from_head(layer_out, 2)
    joined = [jnp.concatenate(line, axis=0) for line in lines([layer_out, opposite])]
    joined, first = lax.optimization_barrier((joined, first))
    beside = near(joined)
    acc = encode(source, [enc_weight[0], first], joined, 0)
    beside, acc, second = lax.optimization_barrier((beside, acc, second))
    encoders = [enc_weight[0], first, second]
    gathered = planes(joined, beside)
    acc = encode(source, encoders, listed(gathered, [0, 1, 2]), 0, late=2, acc=acc)
    acc, layer_out = lax.optimization_barrier((acc, layer_out))
    pooled = encode(source, encoders, listed(gathered, [3]), 3, acc=acc, bias=bias)
    pooled = pooled.astype(jnp.bfloat16)
    pools = pooled.shape[0] // 2
    mine = from_section(pooled[:, : 2 * half])
    first = from_section(pooled[:, 2 * half : 3 * half], paired(0))
    second = from_section(pooled[:, 3 * half :], paired(1))
    after, before = jnp.where(odd, second, first), jnp.where(odd, first, second)
    turned = [
        mine[:pools],
        jnp.concatenate([after[:pools], before[pools:]], axis=1),
        mine[pools:],
        jnp.concatenate([after[pools:], before[:pools]], axis=1),
    ]
    turned = jnp.stack(turned)
    monitor = jnp.concatenate(
        [
            lax.dynamic_index_in_dim(turned, (i - group) % groups, 0, False)
            for i in range(groups)
        ],
        axis=0,
    )
    return (from_section(layer_out[None]), monitor[None])


def solution(mesh):
    return jax.shard_map(
        local,
        mesh=mesh,
        in_specs=(
            P("section", "seq", "head"),
            P("section", "seq", "head"),
            P("section", "seq", "head"),
            P("section", "head", None, None),
            P("section", "seq"),
            P("section", "head"),
            P("section", "head", "seq"),
            P("section", "head", "seq"),
            P("section", None, ("seq", "head")),
            P("section", ("seq", "head")),
        ),
        out_specs=(P("section", "head", "seq"), P("section", None, ("seq", "head"))),
        check_vma=False,
    )
```

```python
import functools

import jax
import jax.numpy as jnp
from jax import lax
from jax.experimental import pallas as pl
from jax.experimental.pallas import tpu as pltpu
from jax.sharding import PartitionSpec as P

HD = 128
POOL = 64
HDIM = 8192
BLK = 128
PACK = 3 * BLK + 16

epsilon = 1e-06
MIB = 1 << 20


def dot(a, b, dims=((1,), (0,))):
    return lax.dot_general(a, b, (dims, ((), ())), preferred_element_type=jnp.float32)


def split(x):
    high = x.astype(jnp.bfloat16)
    return high, (x - high.astype(jnp.float32)).astype(jnp.bfloat16)


def in_hbm(x):
    return pltpu.with_memory_space_constraint(x, pltpu.HBM)


def pack_kernel(queries_ref, keys_ref, values_ref, docs_ref, out_ref):
    docs = jnp.broadcast_to(docs_ref[...].astype(jnp.float32), (PACK - 3 * BLK, BLK))
    docs = docs.astype(out_ref.dtype)
    for head in range(out_ref.shape[0]):
        columns = slice(head * HD, (head + 1) * HD)
        out_ref[head, 0:BLK, :] = queries_ref[:, columns]
        out_ref[head, BLK : 2 * BLK, :] = keys_ref[:, columns]
        out_ref[head, 2 * BLK : 3 * BLK, :] = values_ref[:, columns]
        out_ref[head, 3 * BLK : PACK, :] = docs


def pack(queries, keys, values, docs):
    heads = queries.shape[1] // HD
    return pl.pallas_call(
        pack_kernel,
        out_shape=jax.ShapeDtypeStruct((heads, PACK, HD), jnp.bfloat16),
        compiler_params=pltpu.CompilerParams(vmem_limit_bytes=12 * MIB),
    )(*[in_hbm(x) for x in (queries, keys, values)], docs)


def attend_kernel(packed_ref, prior_ref, gain_ref, out_ref):
    groups, per_group = out_ref.shape[0], packed_ref.shape[0] // out_ref.shape[0]
    row = lax.broadcasted_iota(jnp.int32, (BLK, BLK), 0)
    col = lax.broadcasted_iota(jnp.int32, (BLK, BLK), 1)
    causal = col <= row
    gain = gain_ref[...]
    state = prior_ref[...]
    last = jnp.zeros((BLK, BLK), jnp.float32)
    for group in range(groups):
        for member in range(per_group):
            block = group * per_group + member
            queries = packed_ref[block, 0:BLK, :]
            keys = packed_ref[block, BLK : 2 * BLK, :]
            values = packed_ref[block, 2 * BLK : 3 * BLK, :]
            along = jnp.broadcast_to(
                packed_ref[block, 3 * BLK : PACK, :].astype(jnp.float32)[0:1, :], (BLK, BLK)
            )
            down = along.T
            scores = dot(queries, keys, ((1,), (1,)))
            scores = jnp.where(causal & (along == down), scores, 0.0)
            high, low = split(scores)
            intra = dot(high, values) + dot(low, values)
            high, low = split(state)
            inter = dot(queries, high) + dot(queries, low)
            attended = jnp.where(down == last, inter, 0.0) + intra
            rows = slice(member * BLK, (member + 1) * BLK)
            out_ref[group, rows, :] = (attended * gain).astype(out_ref.dtype)
            newest = jnp.broadcast_to(along[:, BLK - 1 :], (BLK, BLK))
            chosen = jnp.where(down == newest, keys.astype(jnp.float32), 0.0)
            summary = dot(chosen.astype(jnp.bfloat16), values, ((0,), (0,)))
            state = jnp.where(last == newest, state, 0.0) + summary
            last = newest


def attend(packed, prior, gain, groups):
    rows = packed.shape[0] * BLK // groups
    return pl.pallas_call(
        attend_kernel,
        out_shape=jax.ShapeDtypeStruct((groups, rows, HD), jnp.bfloat16),
        compiler_params=pltpu.CompilerParams(vmem_limit_bytes=12 * MIB),
    )(packed, prior, gain)


SLOTS = 2


def listed(gathered, steps):
    return [array for step in steps for parts in gathered for array in parts[step]]


def units(arrays, step, rows):
    parts = [(array, i * rows) for array in arrays for i in range(array.shape[0] // rows)]
    return [(step + n // 8, n // 4 % 2, parts[n : n + 4]) for n in range(0, len(parts), 4)]


def stream(source, work, buffer, sems, fetch, bodies):
    rows, depth = buffer.shape[1], buffer.shape[2] // 4

    def copies(n):
        slot, out = n % SLOTS, []
        for i, (array, first) in enumerate(work[n][2]):
            there = buffer.at[slot, :, i * depth : (i + 1) * depth]
            here = array.at[first : first + rows, :]
            out.append(pltpu.make_async_copy(here, there, sems.at[slot, 0, i]))
        return out

    def start(n):
        for copy in copies(n):
            copy.start()
        for i in range(4):
            fetch(source[(work[n][1] * 4 + work[n][0]) * 4 + i], i, n, True)

    def one(n, body):
        for m in range(1, len(work)):
            pl.when(n + 1 == m)(functools.partial(start, m))
        for m in range(len(work)):

            @pl.when(n == m)
            def _():
                for copy in copies(m):
                    copy.wait()
                for i in range(4):
                    fetch(0, i, m, False)

        half = lax.rem(n, 2)
        row = (half * 4 + work[0][0] + lax.div(n, 2)) * 4
        here = pl.ds(pl.multiple_of(half * rows, BLK), rows)
        body(here, lax.rem(n, SLOTS), [source[row + i] for i in range(4)])

    start(0)
    begin = 0
    for count, body in bodies:

        def step(n, carry, body=body):
            one(n, body)
            return carry

        lax.fori_loop(begin, begin + count, step, 0)
        begin += count


def project_kernel(count, step, final, *refs):
    source, inverse_ref, w0, w1, w2, w3, w4 = refs[:7]
    blocks = refs[7 : 7 + count]
    *rest, buffer, w_buffer, sems = refs[7 + count :]
    if final:
        acc_ref, square_ref, residual_ref, out_ref, acc, square = rest
        acc[...] = acc_ref[...]
        square[...] = square_ref[...]
    else:
        acc, square = rest
        acc[...] = jnp.zeros_like(acc)
        square[...] = jnp.zeros_like(square)
    middle, rows = w2.shape[0] // HD, buffer.shape[1]

    def copy(ref, block, i, k, slot):
        here = pl.ds(pl.multiple_of(block * HD, HD), HD)
        there = w_buffer.at[slot, (4 * i + k) * HD : (4 * i + k + 1) * HD, :]
        return pltpu.make_async_copy(ref.at[here, :], there, sems.at[slot, 1 + k, i])

    def fetch(part, i, n, begin):
        slot = n % SLOTS
        if not begin:
            for k in range(4):
                copy(w0, 0, i, k, slot).wait()
            return
        for k, w in ((0, w0), (1, w1), (3, w4)):
            copy(w, part, i, k, slot).start()

        @pl.when(part < middle)
        def _():
            copy(w2, part, i, 2, slot).start()

        @pl.when(part >= middle)
        def _():
            copy(w3, part - middle, i, 2, slot).start()

    def body(here, slot, parts):
        acc[here, :] += dot(buffer[slot], w_buffer[slot])
        squares = square[here, :]
        width = buffer.shape[2] // 4
        for i, part in enumerate(parts):
            scale = inverse_ref[pl.ds(part, 1), :]
            for j in range(0, width, HD):
                wide = buffer[slot, :, i * width + j : i * width + j + HD].astype(jnp.float32)
                squares += wide * wide * scale[:, j : j + HD]
        square[here, :] = squares

    work = units(blocks, step, rows)
    stream(source, work, buffer, sems, fetch, [(len(work), body)])
    if final:
        mean = jnp.sum(square[...], axis=1, keepdims=True) / HDIM
        scaled = acc[...] * lax.rsqrt(mean + epsilon)
        out_ref[...] = (residual_ref[...].astype(jnp.float32) + scaled).astype(out_ref.dtype)


SMEM, VMEM, HBM, ANY = (
    pl.BlockSpec(memory_space=x) for x in (pltpu.SMEM, pltpu.VMEM, pltpu.HBM, pl.ANY)
)


def project(source, inverse, weights, gathered, residual):
    rows, columns = residual.shape
    depth = gathered[0][0][0].shape[1]
    sums = [
        jax.ShapeDtypeStruct((rows, columns), jnp.float32),
        jax.ShapeDtypeStruct((rows, HD), jnp.float32),
    ]
    slots = [
        pltpu.VMEM((SLOTS, rows // 2, 4 * depth), jnp.bfloat16),
        pltpu.VMEM((SLOTS, 4 * depth, columns), jnp.bfloat16),
        pltpu.SemaphoreType.DMA((SLOTS, 5, 4)),
    ]
    params = pltpu.CompilerParams(vmem_limit_bytes=12 * MIB)
    weights = [in_hbm(w) for w in weights]
    arrays = listed(gathered, [0, 1, 2])
    acc, square = pl.pallas_call(
        functools.partial(project_kernel, len(arrays), 0, False),
        in_specs=[SMEM, VMEM] + [HBM] * 5 + [ANY] * len(arrays),
        out_specs=[VMEM] * 2,
        out_shape=sums,
        scratch_shapes=slots,
        compiler_params=params,
    )(source, inverse, *weights, *arrays)
    arrays = listed(gathered, [3])
    return pl.pallas_call(
        functools.partial(project_kernel, len(arrays), 3, True),
        in_specs=[SMEM, VMEM] + [HBM] * 5 + [ANY] * len(arrays) + [VMEM] * 3,
        out_specs=VMEM,
        out_shape=jax.ShapeDtypeStruct((rows, columns), jnp.bfloat16),
        scratch_shapes=[pltpu.VMEM(x.shape, x.dtype) for x in sums] + slots,
        compiler_params=params,
    )(source, inverse, *weights, *arrays, acc, square, residual)


def encode_kernel(encoder_count, count, step, late, final, *refs):
    source, *encoders = refs[: 1 + encoder_count]
    blocks = refs[1 + encoder_count : 1 + encoder_count + count]
    *rest, buffer, e_buffer, sems = refs[1 + encoder_count + count :]
    if final:
        acc_ref, bias_ref, out_ref, acc = rest
    elif encoder_count == 2:
        (acc,) = rest
        acc_ref = None
    else:
        acc_ref, acc = rest
    acc[...] = jnp.zeros_like(acc) if acc_ref is None else acc_ref[...]
    rows, depth = buffer.shape[1], buffer.shape[2] // 4
    starts = [sum(e.shape[1] for e in encoders[:n]) for n in range(encoder_count + 1)]
    every = list(range(encoder_count))
    work = [(*unit, every[-1:]) for unit in units(blocks[:late], step, rows)]
    work += [(*unit, every) for unit in units(blocks[late:], step + (late > 0), rows)]

    def fetch(part, i, n, begin):
        slot = n % SLOTS
        for k in work[n][3]:
            here = pl.ds(pl.multiple_of(part * depth, BLK), depth)
            to = e_buffer.at[slot, i * depth : (i + 1) * depth, starts[k] : starts[k + 1]]
            copy = pltpu.make_async_copy(encoders[k].at[here, :], to, sems.at[slot, 1 + k, i])
            copy.start() if begin else copy.wait()

    def body(used, here, slot, parts):
        across = slice(starts[used[0]], starts[used[-1] + 1])
        acc[here, across] += dot(buffer[slot], e_buffer[slot, :, across])

    ahead = len(units(blocks[:late], step, rows))
    bodies = [(len(work) - ahead, functools.partial(body, every))]
    if late:
        bodies.insert(0, (ahead, functools.partial(body, every[-1:])))
    stream(source, work, buffer, sems, fetch, bodies)
    if final:
        for i in range(out_ref.shape[0] // 8):
            pools = []
            for j in range(8 * i, 8 * i + 8):
                latent = jnp.maximum(acc[j * POOL : (j + 1) * POOL, :] + bias_ref[...], 0.0)
                pools.append(jnp.sum(latent, axis=0, keepdims=True) * (1.0 / POOL))
            out_ref[8 * i : 8 * i + 8, :] = jnp.concatenate(pools, axis=0)


def encode(source, encoders, arrays, step, late=0, acc=None, bias=None):
    rows, depth = arrays[0].shape[0] // (4 if bias is None else 2), arrays[0].shape[1]
    width = 4 * encoders[1].shape[1]
    shape = jax.ShapeDtypeStruct((2 * rows, width), jnp.float32)
    final = bias is not None
    extra = [x for x in (acc, bias) if x is not None]
    slots = [
        pltpu.VMEM((SLOTS, rows, 4 * depth), jnp.bfloat16),
        pltpu.VMEM((SLOTS, 4 * depth, width), jnp.bfloat16),
        pltpu.SemaphoreType.DMA((SLOTS, 4, 4)),
    ]
    return pl.pallas_call(
        functools.partial(encode_kernel, len(encoders), len(arrays), step, late, final),
        in_specs=[SMEM] + [HBM] * len(encoders) + [ANY] * len(arrays) + [VMEM] * len(extra),
        out_specs=VMEM,
        out_shape=jax.ShapeDtypeStruct((2 * rows // POOL, width), jnp.float32) if final else shape,
        scratch_shapes=([pltpu.VMEM(shape.shape, shape.dtype)] if final else []) + slots,
        compiler_params=pltpu.CompilerParams(vmem_limit_bytes=24 * MIB),
    )(source, *[in_hbm(x) for x in encoders], *arrays, *extra)


SIDE = 4
AXES = (("y", "z"), ("z", "y"))
HOPS = (0, 1, -1, 2)


def moved(x, axis, by):
    pairs = []
    for z in range(SIDE):
        for y in range(SIDE):
            to = (z, (y + by) % SIDE) if axis == "y" else ((z + by) % SIDE, y)
            pairs.append((z * SIDE + y, to[0] * SIDE + to[1]))
    return lax.ppermute(x, "seq", pairs)


def sources(place):
    z, y = place // SIDE, place % SIDE
    table = []
    for axis, _ in AXES:
        for second in HOPS:
            for first in HOPS:
                back_y, back_z = (first, second) if axis == "y" else (second, first)
                table.append((z - back_z) % SIDE * SIDE + (y - back_y) % SIDE)
    return jnp.stack(table).astype(jnp.int32)


def lines(halves):
    return [[half] + [moved(half, axis, by) for by in HOPS[1:]] for half, (axis, _) in zip(halves, AXES)]


def near(joined):
    return [(moved(x, axis, 1), moved(x, axis, -1)) for x, (_, axis) in zip(joined, AXES)]


def planes(joined, beside):
    out = []
    for x, (up, down), (_, axis) in zip(joined, beside, AXES):
        middle = x.shape[0] // 2
        across = (moved(up[:middle], axis, 1), moved(down[middle:], axis, -1))
        out.append(((x,), (up,), (down,), across))
    return out


def local(
    query_vectors,
    key_vectors,
    value_vectors,
    prior_state,
    doc_ids,
    norm_gain,
    residual,
    out_weight,
    enc_weight,
    enc_bias,
):
    groups, sections = lax.axis_size("head"), lax.axis_size("section")
    group, place = lax.axis_index("head"), lax.axis_index("seq")

    def from_head(x, by):
        return lax.ppermute(x, "head", [((i + by) % groups, i) for i in range(groups)])

    def paired(shift):
        pairs = [((i + shift) % groups, (i + 1 + shift) % groups) for i in range(0, groups, 2)]
        return [pair for a, b in pairs for pair in ((a, b), (b, a))]

    def from_section(x, pairs=None):
        both = []
        for s in range(sections):
            for a, b in pairs or [(i, i) for i in range(groups)]:
                both.append((s * groups + a, (s + 1) % sections * groups + b))
        return lax.ppermute(x, ("section", "head"), both)

    packed = pack(query_vectors[0], key_vectors[0], value_vectors[0], doc_ids)
    weight = out_weight[0]
    middle = weight.shape[0] // 2
    after, before = from_head(weight, 1), from_head(weight, -1)
    gains = [norm_gain] + [from_head(norm_gain, k) for k in range(1, groups)]
    inverse = jnp.concatenate([(1.0 / (g * g)).reshape(-1, HD) for g in gains], axis=1)
    half = enc_weight.shape[2] // 2
    odd = group % 2

    def halves(x):
        return [lax.dynamic_slice_in_dim(x, n * half, half, 1) for n in (odd, 1 - odd)]

    first_bias, second_bias = halves(enc_bias)
    bias = jnp.concatenate(
        [
            enc_bias,
            lax.ppermute(first_bias, "head", paired(0)),
            lax.ppermute(second_bias, "head", paired(1)),
        ],
        axis=1,
    )
    source = sources(place)

    packed = lax.all_to_all(packed, "seq", 0, 0, tiled=True)
    first, second = halves(enc_weight[0])
    packed, after, before, inverse, bias, first = lax.optimization_barrier(
        (packed, after, before, inverse, bias, first)
    )
    first = lax.ppermute(first, "head", paired(0))
    prior = lax.dynamic_index_in_dim(prior_state[0], place, 0, False)
    gain = lax.dynamic_slice_in_dim(norm_gain, place * HD, HD, 1)
    attended = attend(packed, prior, gain, groups)

    own = lax.all_to_all(attended, "head", 0, 0, tiled=True)
    own = jnp.concatenate(
        [
            lax.dynamic_index_in_dim(own, (group + k) % groups, 0, False)
            for k in range(groups)
        ],
        axis=1,
    )
    own, *parts = lax.optimization_barrier((own, after[:middle], before[middle:]))
    across = [from_head(parts[0], 1), from_head(parts[1], -1)]
    rows = own.shape[0] // 2
    joined = [jnp.concatenate(line, axis=0) for line in lines([own[:rows], own[rows:]])]
    _, second = lax.optimization_barrier((joined, second))
    second = lax.all_to_all(
        jnp.broadcast_to(second[None], (2, *second.shape)),
        "head",
        0,
        0,
        axis_index_groups=[[(i + 1) % groups, (i + 2) % groups] for i in range(0, groups, 2)],
        tiled=True,
    )
    second = lax.dynamic_index_in_dim(second, odd, 0, False)
    weights = [weight, after, *across, before]
    layer_out = project(source, inverse, weights, planes(joined, near(joined)), residual[0])
    layer_out, first = lax.optimization_barrier((layer_out, first))
    opposite = from_head(layer_out, 2)
    joined = [jnp.concatenate(line, axis=0) for line in lines([layer_out, opposite])]
    beside = near(joined)
    acc = encode(source, [enc_weight[0], first], joined, 0)
    beside, acc, second = lax.optimization_barrier((beside, acc, second))
    encoders = [enc_weight[0], first, second]
    gathered = planes(joined, beside)
    acc = encode(source, encoders, listed(gathered, [0, 1, 2]), 0, late=2, acc=acc)
    acc, layer_out = lax.optimization_barrier((acc, layer_out))
    pooled = encode(source, encoders, listed(gathered, [3]), 3, acc=acc, bias=bias)
    pooled = pooled.astype(jnp.bfloat16)
    pools = pooled.shape[0] // 2
    mine = from_section(pooled[:, : 2 * half])
    first = from_section(pooled[:, 2 * half : 3 * half], paired(0))
    second = from_section(pooled[:, 3 * half :], paired(1))
    after, before = jnp.where(odd, second, first), jnp.where(odd, first, second)
    turned = [
        mine[:pools],
        jnp.concatenate([after[:pools], before[pools:]], axis=1),
        mine[pools:],
        jnp.concatenate([after[pools:], before[:pools]], axis=1),
    ]
    turned = jnp.stack(turned)
    monitor = jnp.concatenate(
        [
            lax.dynamic_index_in_dim(turned, (i - group) % groups, 0, False)
            for i in range(groups)
        ],
        axis=0,
    )
    return (from_section(layer_out[None]), monitor[None])


def solution(mesh):
    return jax.shard_map(
        local,
        mesh=mesh,
        in_specs=(
            P("section", "seq", "head"),
            P("section", "seq", "head"),
            P("section", "seq", "head"),
            P("section", "head", None, None),
            P("section", "seq"),
            P("section", "head"),
            P("section", "head", "seq"),
            P("section", "head", "seq"),
            P("section", None, ("seq", "head")),
            P("section", ("seq", "head")),
        ),
        out_specs=(P("section", "head", "seq"), P("section", None, ("seq", "head"))),
        check_vma=False,
    )
```

```python
import functools

import jax
import jax.numpy as jnp
from jax import lax
from jax.experimental import pallas as pl
from jax.experimental.pallas import tpu as pltpu
from jax.sharding import PartitionSpec as P

HD = 128
POOL = 64
HDIM = 8192
BLK = 128
PACK = 3 * BLK + 16

epsilon = 1e-06
MIB = 1 << 20


def dot(a, b, dims=((1,), (0,))):
    return lax.dot_general(a, b, (dims, ((), ())), preferred_element_type=jnp.float32)


def split(x):
    high = x.astype(jnp.bfloat16)
    return high, (x - high.astype(jnp.float32)).astype(jnp.bfloat16)


def in_hbm(x):
    return pltpu.with_memory_space_constraint(x, pltpu.HBM)


def pack_kernel(queries_ref, keys_ref, values_ref, docs_ref, out_ref):
    docs = jnp.broadcast_to(docs_ref[...].astype(jnp.float32), (PACK - 3 * BLK, BLK))
    docs = docs.astype(out_ref.dtype)
    for head in range(out_ref.shape[0]):
        columns = slice(head * HD, (head + 1) * HD)
        out_ref[head, 0:BLK, :] = queries_ref[:, columns]
        out_ref[head, BLK : 2 * BLK, :] = keys_ref[:, columns]
        out_ref[head, 2 * BLK : 3 * BLK, :] = values_ref[:, columns]
        out_ref[head, 3 * BLK : PACK, :] = docs


def pack(queries, keys, values, docs):
    heads = queries.shape[1] // HD
    return pl.pallas_call(
        pack_kernel,
        out_shape=jax.ShapeDtypeStruct((heads, PACK, HD), jnp.bfloat16),
        compiler_params=pltpu.CompilerParams(vmem_limit_bytes=12 * MIB),
    )(*[in_hbm(x) for x in (queries, keys, values)], docs)


def attend_kernel(packed_ref, prior_ref, gain_ref, out_ref):
    groups, per_group = out_ref.shape[0], packed_ref.shape[0] // out_ref.shape[0]
    row = lax.broadcasted_iota(jnp.int32, (BLK, BLK), 0)
    col = lax.broadcasted_iota(jnp.int32, (BLK, BLK), 1)
    causal = col <= row
    gain = gain_ref[...]
    state = prior_ref[...]
    last = jnp.zeros((BLK, BLK), jnp.float32)
    for group in range(groups):
        for member in range(per_group):
            block = group * per_group + member
            queries = packed_ref[block, 0:BLK, :]
            keys = packed_ref[block, BLK : 2 * BLK, :]
            values = packed_ref[block, 2 * BLK : 3 * BLK, :]
            along = jnp.broadcast_to(
                packed_ref[block, 3 * BLK : PACK, :].astype(jnp.float32)[0:1, :], (BLK, BLK)
            )
            down = along.T
            scores = dot(queries, keys, ((1,), (1,)))
            scores = jnp.where(causal & (along == down), scores, 0.0)
            high, low = split(scores)
            intra = dot(high, values) + dot(low, values)
            high, low = split(state)
            inter = dot(queries, high) + dot(queries, low)
            attended = jnp.where(down == last, inter, 0.0) + intra
            rows = slice(member * BLK, (member + 1) * BLK)
            out_ref[group, rows, :] = (attended * gain).astype(out_ref.dtype)
            newest = jnp.broadcast_to(along[:, BLK - 1 :], (BLK, BLK))
            chosen = jnp.where(down == newest, keys.astype(jnp.float32), 0.0)
            summary = dot(chosen.astype(jnp.bfloat16), values, ((0,), (0,)))
            state = jnp.where(last == newest, state, 0.0) + summary
            last = newest


def attend(packed, prior, gain, groups):
    rows = packed.shape[0] * BLK // groups
    return pl.pallas_call(
        attend_kernel,
        out_shape=jax.ShapeDtypeStruct((groups, rows, HD), jnp.bfloat16),
        compiler_params=pltpu.CompilerParams(vmem_limit_bytes=12 * MIB),
    )(packed, prior, gain)


SLOTS = 2


def listed(gathered, steps):
    return [array for step in steps for parts in gathered for array in parts[step]]


def units(arrays, step, rows):
    parts = [(array, i * rows) for array in arrays for i in range(array.shape[0] // rows)]
    return [(step + n // 8, n // 4 % 2, parts[n : n + 4]) for n in range(0, len(parts), 4)]


def stream(source, work, buffer, sems, fetch, bodies):
    rows, depth = buffer.shape[1], buffer.shape[2] // 4

    def copies(n):
        slot, out = n % SLOTS, []
        for i, (array, first) in enumerate(work[n][2]):
            there = buffer.at[slot, :, i * depth : (i + 1) * depth]
            here = array.at[first : first + rows, :]
            out.append(pltpu.make_async_copy(here, there, sems.at[slot, 0, i]))
        return out

    def start(n):
        for copy in copies(n):
            copy.start()
        for i in range(4):
            fetch(source[(work[n][1] * 4 + work[n][0]) * 4 + i], i, n, True)

    def one(n, body):
        for m in range(1, len(work)):
            pl.when(n + 1 == m)(functools.partial(start, m))
        for m in range(len(work)):

            @pl.when(n == m)
            def _():
                for copy in copies(m):
                    copy.wait()
                for i in range(4):
                    fetch(0, i, m, False)

        half = lax.rem(n, 2)
        row = (half * 4 + work[0][0] + lax.div(n, 2)) * 4
        here = pl.ds(pl.multiple_of(half * rows, BLK), rows)
        body(here, lax.rem(n, SLOTS), [source[row + i] for i in range(4)])

    start(0)
    begin = 0
    for count, body in bodies:

        def step(n, carry, body=body):
            one(n, body)
            return carry

        lax.fori_loop(begin, begin + count, step, 0)
        begin += count


def project_kernel(count, step, final, *refs):
    source, inverse_ref, w0, w1, w2, w3, w4 = refs[:7]
    blocks = refs[7 : 7 + count]
    *rest, buffer, w_buffer, sems = refs[7 + count :]
    if final:
        acc_ref, square_ref, residual_ref, out_ref, acc, square = rest
        acc[...] = acc_ref[...]
        square[...] = square_ref[...]
    else:
        acc, square = rest
        acc[...] = jnp.zeros_like(acc)
        square[...] = jnp.zeros_like(square)
    middle, rows = w2.shape[0] // HD, buffer.shape[1]

    def copy(ref, block, i, k, slot):
        here = pl.ds(pl.multiple_of(block * HD, HD), HD)
        there = w_buffer.at[slot, (4 * i + k) * HD : (4 * i + k + 1) * HD, :]
        return pltpu.make_async_copy(ref.at[here, :], there, sems.at[slot, 1 + k, i])

    def fetch(part, i, n, begin):
        slot = n % SLOTS
        if not begin:
            for k in range(4):
                copy(w0, 0, i, k, slot).wait()
            return
        for k, w in ((0, w0), (1, w1), (3, w4)):
            copy(w, part, i, k, slot).start()

        @pl.when(part < middle)
        def _():
            copy(w2, part, i, 2, slot).start()

        @pl.when(part >= middle)
        def _():
            copy(w3, part - middle, i, 2, slot).start()

    def body(here, slot, parts):
        acc[here, :] += dot(buffer[slot], w_buffer[slot])
        squares = square[here, :]
        width = buffer.shape[2] // 4
        for i, part in enumerate(parts):
            scale = inverse_ref[pl.ds(part, 1), :]
            for j in range(0, width, HD):
                wide = buffer[slot, :, i * width + j : i * width + j + HD].astype(jnp.float32)
                squares += wide * wide * scale[:, j : j + HD]
        square[here, :] = squares

    work = units(blocks, step, rows)
    stream(source, work, buffer, sems, fetch, [(len(work), body)])
    if final:
        mean = jnp.sum(square[...], axis=1, keepdims=True) / HDIM
        scaled = acc[...] * lax.rsqrt(mean + epsilon)
        out_ref[...] = (residual_ref[...].astype(jnp.float32) + scaled).astype(out_ref.dtype)


SMEM, VMEM, HBM, ANY = (
    pl.BlockSpec(memory_space=x) for x in (pltpu.SMEM, pltpu.VMEM, pltpu.HBM, pl.ANY)
)


def project(source, inverse, weights, gathered, residual):
    rows, columns = residual.shape
    depth = gathered[0][0][0].shape[1]
    sums = [
        jax.ShapeDtypeStruct((rows, columns), jnp.float32),
        jax.ShapeDtypeStruct((rows, HD), jnp.float32),
    ]
    slots = [
        pltpu.VMEM((SLOTS, rows // 2, 4 * depth), jnp.bfloat16),
        pltpu.VMEM((SLOTS, 4 * depth, columns), jnp.bfloat16),
        pltpu.SemaphoreType.DMA((SLOTS, 5, 4)),
    ]
    params = pltpu.CompilerParams(vmem_limit_bytes=12 * MIB)
    weights = [in_hbm(w) for w in weights]
    arrays = listed(gathered, [0, 1, 2])
    acc, square = pl.pallas_call(
        functools.partial(project_kernel, len(arrays), 0, False),
        in_specs=[SMEM, VMEM] + [HBM] * 5 + [ANY] * len(arrays),
        out_specs=[VMEM] * 2,
        out_shape=sums,
        scratch_shapes=slots,
        compiler_params=params,
    )(source, inverse, *weights, *arrays)
    arrays = listed(gathered, [3])
    return pl.pallas_call(
        functools.partial(project_kernel, len(arrays), 3, True),
        in_specs=[SMEM, VMEM] + [HBM] * 5 + [ANY] * len(arrays) + [VMEM] * 3,
        out_specs=VMEM,
        out_shape=jax.ShapeDtypeStruct((rows, columns), jnp.bfloat16),
        scratch_shapes=[pltpu.VMEM(x.shape, x.dtype) for x in sums] + slots,
        compiler_params=params,
    )(source, inverse, *weights, *arrays, acc, square, residual)


def encode_kernel(encoder_count, count, step, late, final, *refs):
    source, *encoders = refs[: 1 + encoder_count]
    blocks = refs[1 + encoder_count : 1 + encoder_count + count]
    *rest, buffer, e_buffer, sems = refs[1 + encoder_count + count :]
    if final:
        acc_ref, bias_ref, out_ref, acc = rest
    elif encoder_count == 2:
        (acc,) = rest
        acc_ref = None
    else:
        acc_ref, acc = rest
    acc[...] = jnp.zeros_like(acc) if acc_ref is None else acc_ref[...]
    rows, depth = buffer.shape[1], buffer.shape[2] // 4
    starts = [sum(e.shape[1] for e in encoders[:n]) for n in range(encoder_count + 1)]
    every = list(range(encoder_count))
    work = [(*unit, every[-1:]) for unit in units(blocks[:late], step, rows)]
    work += [(*unit, every) for unit in units(blocks[late:], step + (late > 0), rows)]

    def fetch(part, i, n, begin):
        slot = n % SLOTS
        for k in work[n][3]:
            here = pl.ds(pl.multiple_of(part * depth, BLK), depth)
            to = e_buffer.at[slot, i * depth : (i + 1) * depth, starts[k] : starts[k + 1]]
            copy = pltpu.make_async_copy(encoders[k].at[here, :], to, sems.at[slot, 1 + k, i])
            copy.start() if begin else copy.wait()

    def body(used, here, slot, parts):
        across = slice(starts[used[0]], starts[used[-1] + 1])
        acc[here, across] += dot(buffer[slot], e_buffer[slot, :, across])

    ahead = len(units(blocks[:late], step, rows))
    bodies = [(len(work) - ahead, functools.partial(body, every))]
    if late:
        bodies.insert(0, (ahead, functools.partial(body, every[-1:])))
    stream(source, work, buffer, sems, fetch, bodies)
    if final:
        for i in range(out_ref.shape[0] // 8):
            pools = []
            for j in range(8 * i, 8 * i + 8):
                latent = jnp.maximum(acc[j * POOL : (j + 1) * POOL, :] + bias_ref[...], 0.0)
                pools.append(jnp.sum(latent, axis=0, keepdims=True) * (1.0 / POOL))
            out_ref[8 * i : 8 * i + 8, :] = jnp.concatenate(pools, axis=0)


def encode(source, encoders, arrays, step, late=0, acc=None, bias=None):
    rows, depth = arrays[0].shape[0] // (4 if bias is None else 2), arrays[0].shape[1]
    width = 4 * encoders[1].shape[1]
    shape = jax.ShapeDtypeStruct((2 * rows, width), jnp.float32)
    final = bias is not None
    extra = [x for x in (acc, bias) if x is not None]
    slots = [
        pltpu.VMEM((SLOTS, rows, 4 * depth), jnp.bfloat16),
        pltpu.VMEM((SLOTS, 4 * depth, width), jnp.bfloat16),
        pltpu.SemaphoreType.DMA((SLOTS, 4, 4)),
    ]
    return pl.pallas_call(
        functools.partial(encode_kernel, len(encoders), len(arrays), step, late, final),
        in_specs=[SMEM] + [HBM] * len(encoders) + [ANY] * len(arrays) + [VMEM] * len(extra),
        out_specs=VMEM,
        out_shape=jax.ShapeDtypeStruct((2 * rows // POOL, width), jnp.float32) if final else shape,
        scratch_shapes=([pltpu.VMEM(shape.shape, shape.dtype)] if final else []) + slots,
        compiler_params=pltpu.CompilerParams(vmem_limit_bytes=24 * MIB),
    )(source, *[in_hbm(x) for x in encoders], *arrays, *extra)


SIDE = 4
AXES = (("y", "z"), ("z", "y"))
HOPS = (0, 1, -1, 2)


def moved(x, axis, by):
    pairs = []
    for z in range(SIDE):
        for y in range(SIDE):
            to = (z, (y + by) % SIDE) if axis == "y" else ((z + by) % SIDE, y)
            pairs.append((z * SIDE + y, to[0] * SIDE + to[1]))
    return lax.ppermute(x, "seq", pairs)


def sources(place):
    z, y = place // SIDE, place % SIDE
    table = []
    for axis, _ in AXES:
        for second in HOPS:
            for first in HOPS:
                back_y, back_z = (first, second) if axis == "y" else (second, first)
                table.append((z - back_z) % SIDE * SIDE + (y - back_y) % SIDE)
    return jnp.stack(table).astype(jnp.int32)


def lines(halves):
    return [[half] + [moved(half, axis, by) for by in HOPS[1:]] for half, (axis, _) in zip(halves, AXES)]


def near(joined):
    return [(moved(x, axis, 1), moved(x, axis, -1)) for x, (_, axis) in zip(joined, AXES)]


def planes(joined, beside):
    out = []
    for x, (up, down), (_, axis) in zip(joined, beside, AXES):
        middle = x.shape[0] // 2
        across = (moved(up[:middle], axis, 1), moved(down[middle:], axis, -1))
        out.append(((x,), (up,), (down,), across))
    return out


def local(
    query_vectors,
    key_vectors,
    value_vectors,
    prior_state,
    doc_ids,
    norm_gain,
    residual,
    out_weight,
    enc_weight,
    enc_bias,
):
    groups, sections = lax.axis_size("head"), lax.axis_size("section")
    group, place = lax.axis_index("head"), lax.axis_index("seq")

    def from_head(x, by):
        return lax.ppermute(x, "head", [((i + by) % groups, i) for i in range(groups)])

    def paired(shift):
        pairs = [((i + shift) % groups, (i + 1 + shift) % groups) for i in range(0, groups, 2)]
        return [pair for a, b in pairs for pair in ((a, b), (b, a))]

    def from_section(x, pairs=None):
        both = []
        for s in range(sections):
            for a, b in pairs or [(i, i) for i in range(groups)]:
                both.append((s * groups + a, (s + 1) % sections * groups + b))
        return lax.ppermute(x, ("section", "head"), both)

    packed = pack(query_vectors[0], key_vectors[0], value_vectors[0], doc_ids)
    weight = out_weight[0]
    middle = weight.shape[0] // 2
    after, before = from_head(weight, 1), from_head(weight, -1)
    gains = [norm_gain] + [from_head(norm_gain, k) for k in range(1, groups)]
    inverse = jnp.concatenate([(1.0 / (g * g)).reshape(-1, HD) for g in gains], axis=1)
    half = enc_weight.shape[2] // 2
    odd = group % 2

    def halves(x):
        return [lax.dynamic_slice_in_dim(x, n * half, half, 1) for n in (odd, 1 - odd)]

    first_bias, second_bias = halves(enc_bias)
    bias = jnp.concatenate(
        [
            enc_bias,
            lax.ppermute(first_bias, "head", paired(0)),
            lax.ppermute(second_bias, "head", paired(1)),
        ],
        axis=1,
    )
    source = sources(place)

    packed = lax.all_to_all(packed, "seq", 0, 0, tiled=True)
    first, second = halves(enc_weight[0])
    packed, after, before, inverse, bias, first = lax.optimization_barrier(
        (packed, after, before, inverse, bias, first)
    )
    first = lax.ppermute(first, "head", paired(0))
    prior = lax.dynamic_index_in_dim(prior_state[0], place, 0, False)
    gain = lax.dynamic_slice_in_dim(norm_gain, place * HD, HD, 1)
    attended = attend(packed, prior, gain, groups)

    own = lax.all_to_all(attended, "head", 0, 0, tiled=True)
    own = jnp.concatenate(
        [
            lax.dynamic_index_in_dim(own, (group + k) % groups, 0, False)
            for k in range(groups)
        ],
        axis=1,
    )
    across = [from_head(after[:middle], 1), from_head(before[middle:], -1)]
    own, across = lax.optimization_barrier((own, across))
    rows = own.shape[0] // 2
    joined = [jnp.concatenate(line, axis=0) for line in lines([own[:rows], own[rows:]])]
    *joined, second = lax.optimization_barrier((*joined, second))
    second = lax.all_to_all(
        jnp.broadcast_to(second[None], (2, *second.shape)),
        "head",
        0,
        0,
        axis_index_groups=[[(i + 1) % groups, (i + 2) % groups] for i in range(0, groups, 2)],
        tiled=True,
    )
    second = lax.dynamic_index_in_dim(second, odd, 0, False)
    weights = [weight, after, *across, before]
    layer_out = project(source, inverse, weights, planes(joined, near(joined)), residual[0])
    layer_out, first = lax.optimization_barrier((layer_out, first))
    opposite = from_head(layer_out, 2)
    joined = [jnp.concatenate(line, axis=0) for line in lines([layer_out, opposite])]
    beside = near(joined)
    acc = encode(source, [enc_weight[0], first], joined, 0)
    beside, acc, second = lax.optimization_barrier((beside, acc, second))
    encoders = [enc_weight[0], first, second]
    gathered = planes(joined, beside)
    acc = encode(source, encoders, listed(gathered, [0, 1, 2]), 0, late=2, acc=acc)
    acc, layer_out = lax.optimization_barrier((acc, layer_out))
    pooled = encode(source, encoders, listed(gathered, [3]), 3, acc=acc, bias=bias)
    pooled = pooled.astype(jnp.bfloat16)
    pools = pooled.shape[0] // 2
    mine = from_section(pooled[:, : 2 * half])
    first = from_section(pooled[:, 2 * half : 3 * half], paired(0))
    second = from_section(pooled[:, 3 * half :], paired(1))
    after, before = jnp.where(odd, second, first), jnp.where(odd, first, second)
    turned = [
        mine[:pools],
        jnp.concatenate([after[:pools], before[pools:]], axis=1),
        mine[pools:],
        jnp.concatenate([after[pools:], before[:pools]], axis=1),
    ]
    turned = jnp.stack(turned)
    monitor = jnp.concatenate(
        [
            lax.dynamic_index_in_dim(turned, (i - group) % groups, 0, False)
            for i in range(groups)
        ],
        axis=0,
    )
    return (from_section(layer_out[None]), monitor[None])


def solution(mesh):
    return jax.shard_map(
        local,
        mesh=mesh,
        in_specs=(
            P("section", "seq", "head"),
            P("section", "seq", "head"),
            P("section", "seq", "head"),
            P("section", "head", None, None),
            P("section", "seq"),
            P("section", "head"),
            P("section", "head", "seq"),
            P("section", "head", "seq"),
            P("section", None, ("seq", "head")),
            P("section", ("seq", "head")),
        ),
        out_specs=(P("section", "head", "seq"), P("section", None, ("seq", "head"))),
        check_vma=False,
    )
```

```python
import functools

import jax
import jax.numpy as jnp
from jax import lax
from jax.experimental import pallas as pl
from jax.experimental.pallas import tpu as pltpu
from jax.sharding import PartitionSpec as P

HD = 128
POOL = 64
HDIM = 8192
BLK = 128
PACK = 3 * BLK + 16

epsilon = 1e-06
MIB = 1 << 20


def dot(a, b, dims=((1,), (0,))):
    return lax.dot_general(a, b, (dims, ((), ())), preferred_element_type=jnp.float32)


def split(x):
    high = x.astype(jnp.bfloat16)
    return high, (x - high.astype(jnp.float32)).astype(jnp.bfloat16)


def in_hbm(x):
    return pltpu.with_memory_space_constraint(x, pltpu.HBM)


def pack_kernel(queries_ref, keys_ref, values_ref, docs_ref, out_ref):
    docs = jnp.broadcast_to(docs_ref[...].astype(jnp.float32), (PACK - 3 * BLK, BLK))
    docs = docs.astype(out_ref.dtype)
    for head in range(out_ref.shape[0]):
        columns = slice(head * HD, (head + 1) * HD)
        out_ref[head, 0:BLK, :] = queries_ref[:, columns]
        out_ref[head, BLK : 2 * BLK, :] = keys_ref[:, columns]
        out_ref[head, 2 * BLK : 3 * BLK, :] = values_ref[:, columns]
        out_ref[head, 3 * BLK : PACK, :] = docs


def pack(queries, keys, values, docs):
    heads = queries.shape[1] // HD
    return pl.pallas_call(
        pack_kernel,
        out_shape=jax.ShapeDtypeStruct((heads, PACK, HD), jnp.bfloat16),
        compiler_params=pltpu.CompilerParams(vmem_limit_bytes=12 * MIB),
    )(*[in_hbm(x) for x in (queries, keys, values)], docs)


def attend_kernel(packed_ref, prior_ref, gain_ref, out_ref):
    groups, per_group = out_ref.shape[0], packed_ref.shape[0] // out_ref.shape[0]
    row = lax.broadcasted_iota(jnp.int32, (BLK, BLK), 0)
    col = lax.broadcasted_iota(jnp.int32, (BLK, BLK), 1)
    causal = col <= row
    gain = gain_ref[...]
    state = prior_ref[...]
    last = jnp.zeros((BLK, BLK), jnp.float32)
    for group in range(groups):
        for member in range(per_group):
            block = group * per_group + member
            queries = packed_ref[block, 0:BLK, :]
            keys = packed_ref[block, BLK : 2 * BLK, :]
            values = packed_ref[block, 2 * BLK : 3 * BLK, :]
            along = jnp.broadcast_to(
                packed_ref[block, 3 * BLK : PACK, :].astype(jnp.float32)[0:1, :], (BLK, BLK)
            )
            down = along.T
            scores = dot(queries, keys, ((1,), (1,)))
            scores = jnp.where(causal & (along == down), scores, 0.0)
            high, low = split(scores)
            intra = dot(high, values) + dot(low, values)
            high, low = split(state)
            inter = dot(queries, high) + dot(queries, low)
            attended = jnp.where(down == last, inter, 0.0) + intra
            rows = slice(member * BLK, (member + 1) * BLK)
            out_ref[group, rows, :] = (attended * gain).astype(out_ref.dtype)
            newest = jnp.broadcast_to(along[:, BLK - 1 :], (BLK, BLK))
            chosen = jnp.where(down == newest, keys.astype(jnp.float32), 0.0)
            summary = dot(chosen.astype(jnp.bfloat16), values, ((0,), (0,)))
            state = jnp.where(last == newest, state, 0.0) + summary
            last = newest


def attend(packed, prior, gain, groups):
    rows = packed.shape[0] * BLK // groups
    return pl.pallas_call(
        attend_kernel,
        out_shape=jax.ShapeDtypeStruct((groups, rows, HD), jnp.bfloat16),
        compiler_params=pltpu.CompilerParams(vmem_limit_bytes=12 * MIB),
    )(packed, prior, gain)


SLOTS = 2


def listed(gathered, steps):
    return [array for step in steps for parts in gathered for array in parts[step]]


def units(arrays, step, rows):
    parts = [(array, i * rows) for array in arrays for i in range(array.shape[0] // rows)]
    return [(step + n // 8, n // 4 % 2, parts[n : n + 4]) for n in range(0, len(parts), 4)]


def stream(source, work, buffer, sems, fetch, bodies):
    rows, depth = buffer.shape[1], buffer.shape[2] // 4

    def copies(n):
        slot, out = n % SLOTS, []
        for i, (array, first) in enumerate(work[n][2]):
            there = buffer.at[slot, :, i * depth : (i + 1) * depth]
            here = array.at[first : first + rows, :]
            out.append(pltpu.make_async_copy(here, there, sems.at[slot, 0, i]))
        return out

    def start(n):
        for copy in copies(n):
            copy.start()
        for i in range(4):
            fetch(source[(work[n][1] * 4 + work[n][0]) * 4 + i], i, n, True)

    def one(n, body):
        for m in range(1, len(work)):
            pl.when(n + 1 == m)(functools.partial(start, m))
        for m in range(len(work)):

            @pl.when(n == m)
            def _():
                for copy in copies(m):
                    copy.wait()
                for i in range(4):
                    fetch(0, i, m, False)

        half = lax.rem(n, 2)
        row = (half * 4 + work[0][0] + lax.div(n, 2)) * 4
        here = pl.ds(pl.multiple_of(half * rows, BLK), rows)
        body(here, lax.rem(n, SLOTS), [source[row + i] for i in range(4)])

    start(0)
    begin = 0
    for count, body in bodies:

        def step(n, carry, body=body):
            one(n, body)
            return carry

        lax.fori_loop(begin, begin + count, step, 0)
        begin += count


def project_kernel(count, step, final, *refs):
    source, inverse_ref, w0, w1, w2, w3, w4 = refs[:7]
    blocks = refs[7 : 7 + count]
    *rest, buffer, w_buffer, sems = refs[7 + count :]
    if final:
        acc_ref, square_ref, residual_ref, out_ref, acc, square = rest
        acc[...] = acc_ref[...]
        square[...] = square_ref[...]
    else:
        acc, square = rest
        acc[...] = jnp.zeros_like(acc)
        square[...] = jnp.zeros_like(square)
    middle, rows = w2.shape[0] // HD, buffer.shape[1]

    def copy(ref, block, i, k, slot):
        here = pl.ds(pl.multiple_of(block * HD, HD), HD)
        there = w_buffer.at[slot, (4 * i + k) * HD : (4 * i + k + 1) * HD, :]
        return pltpu.make_async_copy(ref.at[here, :], there, sems.at[slot, 1 + k, i])

    def fetch(part, i, n, begin):
        slot = n % SLOTS
        if not begin:
            for k in range(4):
                copy(w0, 0, i, k, slot).wait()
            return
        for k, w in ((0, w0), (1, w1), (3, w4)):
            copy(w, part, i, k, slot).start()

        @pl.when(part < middle)
        def _():
            copy(w2, part, i, 2, slot).start()

        @pl.when(part >= middle)
        def _():
            copy(w3, part - middle, i, 2, slot).start()

    def body(here, slot, parts):
        acc[here, :] += dot(buffer[slot], w_buffer[slot])
        squares = square[here, :]
        width = buffer.shape[2] // 4
        for i, part in enumerate(parts):
            scale = inverse_ref[pl.ds(part, 1), :]
            for j in range(0, width, HD):
                wide = buffer[slot, :, i * width + j : i * width + j + HD].astype(jnp.float32)
                squares += wide * wide * scale[:, j : j + HD]
        square[here, :] = squares

    work = units(blocks, step, rows)
    stream(source, work, buffer, sems, fetch, [(len(work), body)])
    if final:
        mean = jnp.sum(square[...], axis=1, keepdims=True) / HDIM
        scaled = acc[...] * lax.rsqrt(mean + epsilon)
        out_ref[...] = (residual_ref[...].astype(jnp.float32) + scaled).astype(out_ref.dtype)


SMEM, VMEM, HBM, ANY = (
    pl.BlockSpec(memory_space=x) for x in (pltpu.SMEM, pltpu.VMEM, pltpu.HBM, pl.ANY)
)


def project(source, inverse, weights, gathered, residual):
    rows, columns = residual.shape
    depth = gathered[0][0][0].shape[1]
    sums = [
        jax.ShapeDtypeStruct((rows, columns), jnp.float32),
        jax.ShapeDtypeStruct((rows, HD), jnp.float32),
    ]
    slots = [
        pltpu.VMEM((SLOTS, rows // 2, 4 * depth), jnp.bfloat16),
        pltpu.VMEM((SLOTS, 4 * depth, columns), jnp.bfloat16),
        pltpu.SemaphoreType.DMA((SLOTS, 5, 4)),
    ]
    params = pltpu.CompilerParams(vmem_limit_bytes=12 * MIB)
    weights = [in_hbm(w) for w in weights]
    arrays = listed(gathered, [0, 1, 2])
    acc, square = pl.pallas_call(
        functools.partial(project_kernel, len(arrays), 0, False),
        in_specs=[SMEM, VMEM] + [HBM] * 5 + [ANY] * len(arrays),
        out_specs=[VMEM] * 2,
        out_shape=sums,
        scratch_shapes=slots,
        compiler_params=params,
    )(source, inverse, *weights, *arrays)
    arrays = listed(gathered, [3])
    return pl.pallas_call(
        functools.partial(project_kernel, len(arrays), 3, True),
        in_specs=[SMEM, VMEM] + [HBM] * 5 + [ANY] * len(arrays) + [VMEM] * 3,
        out_specs=VMEM,
        out_shape=jax.ShapeDtypeStruct((rows, columns), jnp.bfloat16),
        scratch_shapes=[pltpu.VMEM(x.shape, x.dtype) for x in sums] + slots,
        compiler_params=params,
    )(source, inverse, *weights, *arrays, acc, square, residual)


def encode_kernel(encoder_count, count, step, late, final, *refs):
    source, *encoders = refs[: 1 + encoder_count]
    blocks = refs[1 + encoder_count : 1 + encoder_count + count]
    *rest, buffer, e_buffer, sems = refs[1 + encoder_count + count :]
    if final:
        acc_ref, bias_ref, out_ref, acc = rest
    elif encoder_count == 2:
        (acc,) = rest
        acc_ref = None
    else:
        acc_ref, acc = rest
    acc[...] = jnp.zeros_like(acc) if acc_ref is None else acc_ref[...]
    rows, depth = buffer.shape[1], buffer.shape[2] // 4
    starts = [sum(e.shape[1] for e in encoders[:n]) for n in range(encoder_count + 1)]
    every = list(range(encoder_count))
    work = [(*unit, every[-1:]) for unit in units(blocks[:late], step, rows)]
    work += [(*unit, every) for unit in units(blocks[late:], step + (late > 0), rows)]

    def fetch(part, i, n, begin):
        slot = n % SLOTS
        for k in work[n][3]:
            here = pl.ds(pl.multiple_of(part * depth, BLK), depth)
            to = e_buffer.at[slot, i * depth : (i + 1) * depth, starts[k] : starts[k + 1]]
            copy = pltpu.make_async_copy(encoders[k].at[here, :], to, sems.at[slot, 1 + k, i])
            copy.start() if begin else copy.wait()

    def body(used, here, slot, parts):
        across = slice(starts[used[0]], starts[used[-1] + 1])
        acc[here, across] += dot(buffer[slot], e_buffer[slot, :, across])

    ahead = len(units(blocks[:late], step, rows))
    bodies = [(len(work) - ahead, functools.partial(body, every))]
    if late:
        bodies.insert(0, (ahead, functools.partial(body, every[-1:])))
    stream(source, work, buffer, sems, fetch, bodies)
    if final:
        for i in range(out_ref.shape[0] // 8):
            pools = []
            for j in range(8 * i, 8 * i + 8):
                latent = jnp.maximum(acc[j * POOL : (j + 1) * POOL, :] + bias_ref[...], 0.0)
                pools.append(jnp.sum(latent, axis=0, keepdims=True) * (1.0 / POOL))
            out_ref[8 * i : 8 * i + 8, :] = jnp.concatenate(pools, axis=0)


def encode(source, encoders, arrays, step, late=0, acc=None, bias=None):
    rows, depth = arrays[0].shape[0] // (4 if bias is None else 2), arrays[0].shape[1]
    width = 4 * encoders[1].shape[1]
    shape = jax.ShapeDtypeStruct((2 * rows, width), jnp.float32)
    final = bias is not None
    extra = [x for x in (acc, bias) if x is not None]
    slots = [
        pltpu.VMEM((SLOTS, rows, 4 * depth), jnp.bfloat16),
        pltpu.VMEM((SLOTS, 4 * depth, width), jnp.bfloat16),
        pltpu.SemaphoreType.DMA((SLOTS, 4, 4)),
    ]
    return pl.pallas_call(
        functools.partial(encode_kernel, len(encoders), len(arrays), step, late, final),
        in_specs=[SMEM] + [HBM] * len(encoders) + [ANY] * len(arrays) + [VMEM] * len(extra),
        out_specs=VMEM,
        out_shape=jax.ShapeDtypeStruct((2 * rows // POOL, width), jnp.float32) if final else shape,
        scratch_shapes=([pltpu.VMEM(shape.shape, shape.dtype)] if final else []) + slots,
        compiler_params=pltpu.CompilerParams(vmem_limit_bytes=24 * MIB),
    )(source, *[in_hbm(x) for x in encoders], *arrays, *extra)


SIDE = 4
AXES = (("y", "z"), ("z", "y"))
HOPS = (0, 1, -1, 2)


def moved(x, axis, by):
    pairs = []
    for z in range(SIDE):
        for y in range(SIDE):
            to = (z, (y + by) % SIDE) if axis == "y" else ((z + by) % SIDE, y)
            pairs.append((z * SIDE + y, to[0] * SIDE + to[1]))
    return lax.ppermute(x, "seq", pairs)


def sources(place):
    z, y = place // SIDE, place % SIDE
    table = []
    for axis, _ in AXES:
        for second in HOPS:
            for first in HOPS:
                back_y, back_z = (first, second) if axis == "y" else (second, first)
                table.append((z - back_z) % SIDE * SIDE + (y - back_y) % SIDE)
    return jnp.stack(table).astype(jnp.int32)


def lines(halves):
    return [[half] + [moved(half, axis, by) for by in HOPS[1:]] for half, (axis, _) in zip(halves, AXES)]


def near(joined):
    return [(moved(x, axis, 1), moved(x, axis, -1)) for x, (_, axis) in zip(joined, AXES)]


def planes(joined, beside):
    out = []
    for x, (up, down), (_, axis) in zip(joined, beside, AXES):
        middle = x.shape[0] // 2
        across = (moved(up[:middle], axis, 1), moved(down[middle:], axis, -1))
        out.append(((x,), (up,), (down,), across))
    return out


def local(
    query_vectors,
    key_vectors,
    value_vectors,
    prior_state,
    doc_ids,
    norm_gain,
    residual,
    out_weight,
    enc_weight,
    enc_bias,
):
    groups, sections = lax.axis_size("head"), lax.axis_size("section")
    group, place = lax.axis_index("head"), lax.axis_index("seq")

    def from_head(x, by):
        return lax.ppermute(x, "head", [((i + by) % groups, i) for i in range(groups)])

    def paired(shift):
        pairs = [((i + shift) % groups, (i + 1 + shift) % groups) for i in range(0, groups, 2)]
        return [pair for a, b in pairs for pair in ((a, b), (b, a))]

    def from_section(x, pairs=None):
        both = []
        for s in range(sections):
            for a, b in pairs or [(i, i) for i in range(groups)]:
                both.append((s * groups + a, (s + 1) % sections * groups + b))
        return lax.ppermute(x, ("section", "head"), both)

    packed = pack(query_vectors[0], key_vectors[0], value_vectors[0], doc_ids)
    weight = out_weight[0]
    middle = weight.shape[0] // 2
    after, before = from_head(weight, 1), from_head(weight, -1)
    gains = [norm_gain] + [from_head(norm_gain, k) for k in range(1, groups)]
    inverse = jnp.concatenate([(1.0 / (g * g)).reshape(-1, HD) for g in gains], axis=1)
    half = enc_weight.shape[2] // 2
    odd = group % 2

    def halves(x):
        return [lax.dynamic_slice_in_dim(x, n * half, half, 1) for n in (odd, 1 - odd)]

    first_bias, second_bias = halves(enc_bias)
    bias = jnp.concatenate(
        [
            enc_bias,
            lax.ppermute(second_bias, "head", paired(1)),
            lax.ppermute(first_bias, "head", paired(0)),
        ],
        axis=1,
    )
    source = sources(place)

    packed = lax.all_to_all(packed, "seq", 0, 0, tiled=True)
    first, second = halves(enc_weight[0])
    packed, after, before, inverse, bias = lax.optimization_barrier(
        (packed, after, before, inverse, bias)
    )
    prior = lax.dynamic_index_in_dim(prior_state[0], place, 0, False)
    gain = lax.dynamic_slice_in_dim(norm_gain, place * HD, HD, 1)
    attended = attend(packed, prior, gain, groups)

    own = lax.all_to_all(attended, "head", 0, 0, tiled=True)
    own = jnp.concatenate(
        [
            lax.dynamic_index_in_dim(own, (group + k) % groups, 0, False)
            for k in range(groups)
        ],
        axis=1,
    )
    own, *parts = lax.optimization_barrier((own, after[:middle], before[middle:]))
    across = [from_head(parts[0], 1), from_head(parts[1], -1)]
    rows = own.shape[0] // 2
    joined = [jnp.concatenate(line, axis=0) for line in lines([own[:rows], own[rows:]])]
    _, across, second = lax.optimization_barrier((joined, across, second))
    second = lax.all_to_all(
        jnp.broadcast_to(second[None], (2, *second.shape)),
        "head",
        0,
        0,
        axis_index_groups=[[(i + 1) % groups, (i + 2) % groups] for i in range(0, groups, 2)],
        tiled=True,
    )
    second = lax.dynamic_index_in_dim(second, odd, 0, False)
    weights = [weight, after, *across, before]
    layer_out = project(source, inverse, weights, planes(joined, near(joined)), residual[0])
    opposite = from_head(layer_out, 2)
    opposite, first = lax.optimization_barrier((opposite, first))
    first = lax.ppermute(first, "head", paired(0))
    joined = [jnp.concatenate(line, axis=0) for line in lines([layer_out, opposite])]
    beside = near(joined)
    acc = encode(source, [enc_weight[0], second], joined, 0)
    beside, acc = lax.optimization_barrier((beside, acc))
    encoders = [enc_weight[0], second, first]
    gathered = planes(joined, beside)
    acc = encode(source, encoders, listed(gathered, [0, 1, 2]), 0, late=2, acc=acc)
    acc, layer_out = lax.optimization_barrier((acc, layer_out))
    pooled = encode(source, encoders, listed(gathered, [3]), 3, acc=acc, bias=bias)
    pooled = pooled.astype(jnp.bfloat16)
    pools = pooled.shape[0] // 2
    mine = from_section(pooled[:, : 2 * half])
    second = from_section(pooled[:, 2 * half : 3 * half], paired(1))
    first = from_section(pooled[:, 3 * half :], paired(0))
    after, before = jnp.where(odd, second, first), jnp.where(odd, first, second)
    turned = [
        mine[:pools],
        jnp.concatenate([after[:pools], before[pools:]], axis=1),
        mine[pools:],
        jnp.concatenate([after[pools:], before[:pools]], axis=1),
    ]
    turned = jnp.stack(turned)
    monitor = jnp.concatenate(
        [
            lax.dynamic_index_in_dim(turned, (i - group) % groups, 0, False)
            for i in range(groups)
        ],
        axis=0,
    )
    return (from_section(layer_out[None]), monitor[None])


def solution(mesh):
    return jax.shard_map(
        local,
        mesh=mesh,
        in_specs=(
            P("section", "seq", "head"),
            P("section", "seq", "head"),
            P("section", "seq", "head"),
            P("section", "head", None, None),
            P("section", "seq"),
            P("section", "head"),
            P("section", "head", "seq"),
            P("section", "head", "seq"),
            P("section", None, ("seq", "head")),
            P("section", ("seq", "head")),
        ),
        out_specs=(P("section", "head", "seq"), P("section", None, ("seq", "head"))),
        check_vma=False,
    )
```

```python
import functools

import jax
import jax.numpy as jnp
from jax import lax
from jax.experimental import pallas as pl
from jax.experimental.pallas import tpu as pltpu
from jax.sharding import PartitionSpec as P

HD = 128
POOL = 64
HDIM = 8192
BLK = 128
PACK = 3 * BLK + 16

epsilon = 1e-06
MIB = 1 << 20


def dot(a, b, dims=((1,), (0,))):
    return lax.dot_general(a, b, (dims, ((), ())), preferred_element_type=jnp.float32)


def split(x):
    high = x.astype(jnp.bfloat16)
    return high, (x - high.astype(jnp.float32)).astype(jnp.bfloat16)


def in_hbm(x):
    return pltpu.with_memory_space_constraint(x, pltpu.HBM)


def pack_kernel(queries_ref, keys_ref, values_ref, docs_ref, out_ref):
    docs = jnp.broadcast_to(docs_ref[...].astype(jnp.float32), (PACK - 3 * BLK, BLK))
    docs = docs.astype(out_ref.dtype)
    for head in range(out_ref.shape[0]):
        columns = slice(head * HD, (head + 1) * HD)
        out_ref[head, 0:BLK, :] = queries_ref[:, columns]
        out_ref[head, BLK : 2 * BLK, :] = keys_ref[:, columns]
        out_ref[head, 2 * BLK : 3 * BLK, :] = values_ref[:, columns]
        out_ref[head, 3 * BLK : PACK, :] = docs


def pack(queries, keys, values, docs):
    heads = queries.shape[1] // HD
    return pl.pallas_call(
        pack_kernel,
        out_shape=jax.ShapeDtypeStruct((heads, PACK, HD), jnp.bfloat16),
        compiler_params=pltpu.CompilerParams(vmem_limit_bytes=12 * MIB),
    )(*[in_hbm(x) for x in (queries, keys, values)], docs)


def attend_kernel(packed_ref, prior_ref, gain_ref, out_ref):
    groups, per_group = out_ref.shape[0], packed_ref.shape[0] // out_ref.shape[0]
    row = lax.broadcasted_iota(jnp.int32, (BLK, BLK), 0)
    col = lax.broadcasted_iota(jnp.int32, (BLK, BLK), 1)
    causal = col <= row
    gain = gain_ref[...]
    state = prior_ref[...]
    last = jnp.zeros((BLK, BLK), jnp.float32)
    for group in range(groups):
        for member in range(per_group):
            block = group * per_group + member
            queries = packed_ref[block, 0:BLK, :]
            keys = packed_ref[block, BLK : 2 * BLK, :]
            values = packed_ref[block, 2 * BLK : 3 * BLK, :]
            along = jnp.broadcast_to(
                packed_ref[block, 3 * BLK : PACK, :].astype(jnp.float32)[0:1, :], (BLK, BLK)
            )
            down = along.T
            scores = dot(queries, keys, ((1,), (1,)))
            scores = jnp.where(causal & (along == down), scores, 0.0)
            high, low = split(scores)
            intra = dot(high, values) + dot(low, values)
            high, low = split(state)
            inter = dot(queries, high) + dot(queries, low)
            attended = jnp.where(down == last, inter, 0.0) + intra
            rows = slice(member * BLK, (member + 1) * BLK)
            out_ref[group, rows, :] = (attended * gain).astype(out_ref.dtype)
            newest = jnp.broadcast_to(along[:, BLK - 1 :], (BLK, BLK))
            chosen = jnp.where(down == newest, keys.astype(jnp.float32), 0.0)
            summary = dot(chosen.astype(jnp.bfloat16), values, ((0,), (0,)))
            state = jnp.where(last == newest, state, 0.0) + summary
            last = newest


def attend(packed, prior, gain, groups):
    rows = packed.shape[0] * BLK // groups
    return pl.pallas_call(
        attend_kernel,
        out_shape=jax.ShapeDtypeStruct((groups, rows, HD), jnp.bfloat16),
        compiler_params=pltpu.CompilerParams(vmem_limit_bytes=12 * MIB),
    )(packed, prior, gain)


SLOTS = 2


def listed(gathered, steps):
    return [array for step in steps for parts in gathered for array in parts[step]]


def units(arrays, step, rows):
    parts = [(array, i * rows) for array in arrays for i in range(array.shape[0] // rows)]
    return [(step + n // 8, n // 4 % 2, parts[n : n + 4]) for n in range(0, len(parts), 4)]


def stream(source, work, buffer, sems, fetch, bodies):
    rows, depth = buffer.shape[1], buffer.shape[2] // 4

    def copies(n):
        slot, out = n % SLOTS, []
        for i, (array, first) in enumerate(work[n][2]):
            there = buffer.at[slot, :, i * depth : (i + 1) * depth]
            here = array.at[first : first + rows, :]
            out.append(pltpu.make_async_copy(here, there, sems.at[slot, 0, i]))
        return out

    def start(n):
        for copy in copies(n):
            copy.start()
        for i in range(4):
            fetch(source[(work[n][1] * 4 + work[n][0]) * 4 + i], i, n, True)

    def one(n, body):
        for m in range(1, len(work)):
            pl.when(n + 1 == m)(functools.partial(start, m))
        for m in range(len(work)):

            @pl.when(n == m)
            def _():
                for copy in copies(m):
                    copy.wait()
                for i in range(4):
                    fetch(0, i, m, False)

        half = lax.rem(n, 2)
        row = (half * 4 + work[0][0] + lax.div(n, 2)) * 4
        here = pl.ds(pl.multiple_of(half * rows, BLK), rows)
        body(here, lax.rem(n, SLOTS), [source[row + i] for i in range(4)])

    start(0)
    begin = 0
    for count, body in bodies:

        def step(n, carry, body=body):
            one(n, body)
            return carry

        lax.fori_loop(begin, begin + count, step, 0)
        begin += count


def project_kernel(count, step, final, *refs):
    source, inverse_ref, w0, w1, w2, w3, w4 = refs[:7]
    blocks = refs[7 : 7 + count]
    *rest, buffer, w_buffer, sems = refs[7 + count :]
    if final:
        acc_ref, square_ref, residual_ref, out_ref, acc, square = rest
        acc[...] = acc_ref[...]
        square[...] = square_ref[...]
    else:
        acc, square = rest
        acc[...] = jnp.zeros_like(acc)
        square[...] = jnp.zeros_like(square)
    middle, rows = w2.shape[0] // HD, buffer.shape[1]

    def copy(ref, block, i, k, slot):
        here = pl.ds(pl.multiple_of(block * HD, HD), HD)
        there = w_buffer.at[slot, (4 * i + k) * HD : (4 * i + k + 1) * HD, :]
        return pltpu.make_async_copy(ref.at[here, :], there, sems.at[slot, 1 + k, i])

    def fetch(part, i, n, begin):
        slot = n % SLOTS
        if not begin:
            for k in range(4):
                copy(w0, 0, i, k, slot).wait()
            return
        for k, w in ((0, w0), (1, w1), (3, w4)):
            copy(w, part, i, k, slot).start()

        @pl.when(part < middle)
        def _():
            copy(w2, part, i, 2, slot).start()

        @pl.when(part >= middle)
        def _():
            copy(w3, part - middle, i, 2, slot).start()

    def body(here, slot, parts):
        acc[here, :] += dot(buffer[slot], w_buffer[slot])
        squares = square[here, :]
        width = buffer.shape[2] // 4
        for i, part in enumerate(parts):
            scale = inverse_ref[pl.ds(part, 1), :]
            for j in range(0, width, HD):
                wide = buffer[slot, :, i * width + j : i * width + j + HD].astype(jnp.float32)
                squares += wide * wide * scale[:, j : j + HD]
        square[here, :] = squares

    work = units(blocks, step, rows)
    stream(source, work, buffer, sems, fetch, [(len(work), body)])
    if final:
        mean = jnp.sum(square[...], axis=1, keepdims=True) / HDIM
        scaled = acc[...] * lax.rsqrt(mean + epsilon)
        out_ref[...] = (residual_ref[...].astype(jnp.float32) + scaled).astype(out_ref.dtype)


SMEM, VMEM, HBM, ANY = (
    pl.BlockSpec(memory_space=x) for x in (pltpu.SMEM, pltpu.VMEM, pltpu.HBM, pl.ANY)
)


def project(source, inverse, weights, gathered, residual):
    rows, columns = residual.shape
    depth = gathered[0][0][0].shape[1]
    sums = [
        jax.ShapeDtypeStruct((rows, columns), jnp.float32),
        jax.ShapeDtypeStruct((rows, HD), jnp.float32),
    ]
    slots = [
        pltpu.VMEM((SLOTS, rows // 2, 4 * depth), jnp.bfloat16),
        pltpu.VMEM((SLOTS, 4 * depth, columns), jnp.bfloat16),
        pltpu.SemaphoreType.DMA((SLOTS, 5, 4)),
    ]
    params = pltpu.CompilerParams(vmem_limit_bytes=12 * MIB)
    weights = [in_hbm(w) for w in weights]
    arrays = listed(gathered, [0, 1, 2])
    acc, square = pl.pallas_call(
        functools.partial(project_kernel, len(arrays), 0, False),
        in_specs=[SMEM, VMEM] + [HBM] * 5 + [ANY] * len(arrays),
        out_specs=[VMEM] * 2,
        out_shape=sums,
        scratch_shapes=slots,
        compiler_params=params,
    )(source, inverse, *weights, *arrays)
    arrays = listed(gathered, [3])
    return pl.pallas_call(
        functools.partial(project_kernel, len(arrays), 3, True),
        in_specs=[SMEM, VMEM] + [HBM] * 5 + [ANY] * len(arrays) + [VMEM] * 3,
        out_specs=VMEM,
        out_shape=jax.ShapeDtypeStruct((rows, columns), jnp.bfloat16),
        scratch_shapes=[pltpu.VMEM(x.shape, x.dtype) for x in sums] + slots,
        compiler_params=params,
    )(source, inverse, *weights, *arrays, acc, square, residual)


def encode_kernel(encoder_count, count, step, late, final, *refs):
    source, *encoders = refs[: 1 + encoder_count]
    blocks = refs[1 + encoder_count : 1 + encoder_count + count]
    *rest, buffer, e_buffer, sems = refs[1 + encoder_count + count :]
    if final:
        acc_ref, bias_ref, out_ref, acc = rest
    elif encoder_count == 2:
        (acc,) = rest
        acc_ref = None
    else:
        acc_ref, acc = rest
    acc[...] = jnp.zeros_like(acc) if acc_ref is None else acc_ref[...]
    rows, depth = buffer.shape[1], buffer.shape[2] // 4
    starts = [sum(e.shape[1] for e in encoders[:n]) for n in range(encoder_count + 1)]
    every = list(range(encoder_count))
    work = [(*unit, every[-1:]) for unit in units(blocks[:late], step, rows)]
    work += [(*unit, every) for unit in units(blocks[late:], step + (late > 0), rows)]

    def fetch(part, i, n, begin):
        slot = n % SLOTS
        for k in work[n][3]:
            here = pl.ds(pl.multiple_of(part * depth, BLK), depth)
            to = e_buffer.at[slot, i * depth : (i + 1) * depth, starts[k] : starts[k + 1]]
            copy = pltpu.make_async_copy(encoders[k].at[here, :], to, sems.at[slot, 1 + k, i])
            copy.start() if begin else copy.wait()

    def body(used, here, slot, parts):
        across = slice(starts[used[0]], starts[used[-1] + 1])
        acc[here, across] += dot(buffer[slot], e_buffer[slot, :, across])

    ahead = len(units(blocks[:late], step, rows))
    bodies = [(len(work) - ahead, functools.partial(body, every))]
    if late:
        bodies.insert(0, (ahead, functools.partial(body, every[-1:])))
    stream(source, work, buffer, sems, fetch, bodies)
    if final:
        for i in range(out_ref.shape[0] // 8):
            pools = []
            for j in range(8 * i, 8 * i + 8):
                latent = jnp.maximum(acc[j * POOL : (j + 1) * POOL, :] + bias_ref[...], 0.0)
                pools.append(jnp.sum(latent, axis=0, keepdims=True) * (1.0 / POOL))
            out_ref[8 * i : 8 * i + 8, :] = jnp.concatenate(pools, axis=0)


def encode(source, encoders, arrays, step, late=0, acc=None, bias=None):
    rows, depth = arrays[0].shape[0] // (4 if bias is None else 2), arrays[0].shape[1]
    width = 4 * encoders[1].shape[1]
    shape = jax.ShapeDtypeStruct((2 * rows, width), jnp.float32)
    final = bias is not None
    extra = [x for x in (acc, bias) if x is not None]
    slots = [
        pltpu.VMEM((SLOTS, rows, 4 * depth), jnp.bfloat16),
        pltpu.VMEM((SLOTS, 4 * depth, width), jnp.bfloat16),
        pltpu.SemaphoreType.DMA((SLOTS, 4, 4)),
    ]
    return pl.pallas_call(
        functools.partial(encode_kernel, len(encoders), len(arrays), step, late, final),
        in_specs=[SMEM] + [HBM] * len(encoders) + [ANY] * len(arrays) + [VMEM] * len(extra),
        out_specs=VMEM,
        out_shape=jax.ShapeDtypeStruct((2 * rows // POOL, width), jnp.float32) if final else shape,
        scratch_shapes=([pltpu.VMEM(shape.shape, shape.dtype)] if final else []) + slots,
        compiler_params=pltpu.CompilerParams(vmem_limit_bytes=24 * MIB),
    )(source, *[in_hbm(x) for x in encoders], *arrays, *extra)


SIDE = 4
AXES = (("y", "z"), ("z", "y"))
HOPS = (0, 1, -1, 2)


def moved(x, axis, by):
    pairs = []
    for z in range(SIDE):
        for y in range(SIDE):
            to = (z, (y + by) % SIDE) if axis == "y" else ((z + by) % SIDE, y)
            pairs.append((z * SIDE + y, to[0] * SIDE + to[1]))
    return lax.ppermute(x, "seq", pairs)


def sources(place):
    z, y = place // SIDE, place % SIDE
    table = []
    for axis, _ in AXES:
        for second in HOPS:
            for first in HOPS:
                back_y, back_z = (first, second) if axis == "y" else (second, first)
                table.append((z - back_z) % SIDE * SIDE + (y - back_y) % SIDE)
    return jnp.stack(table).astype(jnp.int32)


def lines(halves):
    return [[half] + [moved(half, axis, by) for by in HOPS[1:]] for half, (axis, _) in zip(halves, AXES)]


def near(joined):
    return [(moved(x, axis, 1), moved(x, axis, -1)) for x, (_, axis) in zip(joined, AXES)]


def planes(joined, beside):
    out = []
    for x, (up, down), (_, axis) in zip(joined, beside, AXES):
        middle = x.shape[0] // 2
        across = (moved(up[:middle], axis, 1), moved(down[middle:], axis, -1))
        out.append(((x,), (up,), (down,), across))
    return out


def local(
    query_vectors,
    key_vectors,
    value_vectors,
    prior_state,
    doc_ids,
    norm_gain,
    residual,
    out_weight,
    enc_weight,
    enc_bias,
):
    groups, sections = lax.axis_size("head"), lax.axis_size("section")
    group, place = lax.axis_index("head"), lax.axis_index("seq")

    def from_head(x, by):
        return lax.ppermute(x, "head", [((i + by) % groups, i) for i in range(groups)])

    def paired(shift):
        pairs = [((i + shift) % groups, (i + 1 + shift) % groups) for i in range(0, groups, 2)]
        return [pair for a, b in pairs for pair in ((a, b), (b, a))]

    def from_section(x, pairs=None):
        both = []
        for s in range(sections):
            for a, b in pairs or [(i, i) for i in range(groups)]:
                both.append((s * groups + a, (s + 1) % sections * groups + b))
        return lax.ppermute(x, ("section", "head"), both)

    packed = pack(query_vectors[0], key_vectors[0], value_vectors[0], doc_ids)
    weight = out_weight[0]
    middle = weight.shape[0] // 2
    after, before = from_head(weight, 1), from_head(weight, -1)
    gains = [norm_gain] + [from_head(norm_gain, k) for k in range(1, groups)]
    inverse = jnp.concatenate([(1.0 / (g * g)).reshape(-1, HD) for g in gains], axis=1)
    half = enc_weight.shape[2] // 2
    odd = group % 2

    def halves(x):
        return [lax.dynamic_slice_in_dim(x, n * half, half, 1) for n in (odd, 1 - odd)]

    first_bias, second_bias = halves(enc_bias)
    packed, first_bias, second_bias = lax.optimization_barrier((packed, first_bias, second_bias))
    bias = jnp.concatenate(
        [
            enc_bias,
            lax.ppermute(second_bias, "head", paired(1)),
            lax.ppermute(first_bias, "head", paired(0)),
        ],
        axis=1,
    )
    source = sources(place)

    packed = lax.all_to_all(packed, "seq", 0, 0, tiled=True)
    first, second = halves(enc_weight[0])
    packed, after, before, inverse, bias = lax.optimization_barrier(
        (packed, after, before, inverse, bias)
    )
    prior = lax.dynamic_index_in_dim(prior_state[0], place, 0, False)
    gain = lax.dynamic_slice_in_dim(norm_gain, place * HD, HD, 1)
    attended = attend(packed, prior, gain, groups)

    own = lax.all_to_all(attended, "head", 0, 0, tiled=True)
    own = jnp.concatenate(
        [
            lax.dynamic_index_in_dim(own, (group + k) % groups, 0, False)
            for k in range(groups)
        ],
        axis=1,
    )
    own, *parts = lax.optimization_barrier((own, after[:middle], before[middle:]))
    across = [from_head(parts[0], 1), from_head(parts[1], -1)]
    rows = own.shape[0] // 2
    joined = [jnp.concatenate(line, axis=0) for line in lines([own[:rows], own[rows:]])]
    _, across, second = lax.optimization_barrier((joined, across, second))
    second = lax.all_to_all(
        jnp.broadcast_to(second[None], (2, *second.shape)),
        "head",
        0,
        0,
        axis_index_groups=[[(i + 1) % groups, (i + 2) % groups] for i in range(0, groups, 2)],
        tiled=True,
    )
    second = lax.dynamic_index_in_dim(second, odd, 0, False)
    weights = [weight, after, *across, before]
    layer_out = project(source, inverse, weights, planes(joined, near(joined)), residual[0])
    opposite = from_head(layer_out, 2)
    opposite, first = lax.optimization_barrier((opposite, first))
    first = lax.ppermute(first, "head", paired(0))
    joined = [jnp.concatenate(line, axis=0) for line in lines([layer_out, opposite])]
    beside = near(joined)
    acc = encode(source, [enc_weight[0], second], joined, 0)
    beside, acc = lax.optimization_barrier((beside, acc))
    encoders = [enc_weight[0], second, first]
    gathered = planes(joined, beside)
    acc = encode(source, encoders, listed(gathered, [0, 1, 2]), 0, late=2, acc=acc)
    acc, layer_out = lax.optimization_barrier((acc, layer_out))
    pooled = encode(source, encoders, listed(gathered, [3]), 3, acc=acc, bias=bias)
    pooled = pooled.astype(jnp.bfloat16)
    pools = pooled.shape[0] // 2
    mine = from_section(pooled[:, : 2 * half])
    second = from_section(pooled[:, 2 * half : 3 * half], paired(1))
    first = from_section(pooled[:, 3 * half :], paired(0))
    after, before = jnp.where(odd, second, first), jnp.where(odd, first, second)
    turned = [
        mine[:pools],
        jnp.concatenate([after[:pools], before[pools:]], axis=1),
        mine[pools:],
        jnp.concatenate([after[pools:], before[:pools]], axis=1),
    ]
    turned = jnp.stack(turned)
    monitor = jnp.concatenate(
        [
            lax.dynamic_index_in_dim(turned, (i - group) % groups, 0, False)
            for i in range(groups)
        ],
        axis=0,
    )
    return (from_section(layer_out[None]), monitor[None])


def solution(mesh):
    return jax.shard_map(
        local,
        mesh=mesh,
        in_specs=(
            P("section", "seq", "head"),
            P("section", "seq", "head"),
            P("section", "seq", "head"),
            P("section", "head", None, None),
            P("section", "seq"),
            P("section", "head"),
            P("section", "head", "seq"),
            P("section", "head", "seq"),
            P("section", None, ("seq", "head")),
            P("section", ("seq", "head")),
        ),
        out_specs=(P("section", "head", "seq"), P("section", None, ("seq", "head"))),
        check_vma=False,
    )
```
